32 devices in a mesh: ja: 4 (over x, core), ka: 8 (over z, y).
Axes of the slice: x: 2, y: 2, z: 4, core: 2. Of those that a mesh axis runs over, the one named last changes fastest.
Arguments:
- blocks: bfloat16 [1024, 64, 4096], P(('ja', 'ka')), may hold values from -6 to 6
- factor_b: bfloat16 [2048, 256], P('ja'), may hold values from -0.3984375 to 0.3984375
- factor_c: bfloat16 [2048, 256], P('ka'), may hold values from -0.3984375 to 0.3984375
- block_coords: int32 [1024, 3], P(('ja', 'ka')), may hold values from 0 to 31, as said below
- block_count: int32 [32], P(('ja', 'ka')), may hold values from 1 to 31, as said below
Outputs:
- new_factor: float32 [2048, 256], P(('ja', 'ka'))
The draws below stay inside these ranges and needn't reach their ends.
Inputs may be any that keep to these rules, and one draw needn't show every extreme that they name: `block_coords`: column 0 lies in 0 to 1 * 32 - 1 and is different for every slot of one device, column 1 in 0 to 7, column 2 in 0 to 3. `block_count`: a device and the device whose ka index lies half the ka axis away hold 32 live slots together; a device's live slots are its first ones.
All inputs are finite; a program needn't handle non-finite values.
Results may differ from the reference program's by a relative error of at most 0.0041.
Values may be sent and summed in bfloat16 or wider, within the bound.
No kernel may reach another device: no remote copies, remote signals or barrier semaphores. Data moves between devices by JAX's collectives and lax.ppermute only.
A program may use at most 128 MiB of HBM per device.

```python
import jax
import jax.numpy as jnp
from jax import lax

RANK = 256
EDGE = 64
SLOTS = 32
FIRST_DEV = 1
SECOND_DEV = 8
THIRD_DEV = 4
BLOCKS = 1024
SECOND = 2048
THIRD = 2048
N_JA = 4
N_KA = 8
DEVICES = 32


def draw_block_coords(key, part):
    keys = jax.random.split(jax.random.fold_in(key, 7), 3)
    owner_keys = jax.random.split(keys[0], DEVICES)

    def owners(one_key):
        return jax.random.permutation(one_key, FIRST_DEV * DEVICES)[:SLOTS]
    first = jax.vmap(owners)(owner_keys).reshape(-1)
    second = jax.random.randint(keys[1], (BLOCKS,), 0, SECOND_DEV)
    third = jax.random.randint(keys[2], (BLOCKS,), 0, THIRD_DEV)
    return jnp.stack([first, second, third], axis=1).astype(jnp.int32)


def draw_block_count(key, part):
    halfway = N_KA // 2
    lower = jax.random.randint(jax.random.fold_in(key, 11), (DEVICES,), 1, SLOTS)
    lower = lower.at[0].set(SLOTS - 1)
    index = jnp.arange(DEVICES)
    partner = jnp.bitwise_xor(index, halfway)
    in_lower = index % N_KA < halfway
    return jnp.where(in_lower, lower, SLOTS - lower[partner]).astype(jnp.int32)


def shard_levels(own_key, shape, pieces, least, high):
    loudness, own = 1.0, jax.random.fold_in(own_key, 6)
    for dim, parts in pieces:
        heights = jnp.exp(jax.random.uniform(jax.random.fold_in(own, dim), (parts,), jnp.float32, least / len(pieces), high / len(pieces)))
        loudness = loudness * jnp.repeat(heights, shape[dim] // parts).reshape([-1 if axis == dim else 1 for axis in range(len(shape))])
    return loudness


def noise(stream_key, extent, scale, limit, pieces=(), held_as=jnp.bfloat16):
    array = jax.random.normal(stream_key, extent, jnp.float32) * scale
    if len(pieces) > 0:
        array = shard_levels(stream_key, extent, pieces, -0.22, 0.18) * array
    return jnp.clip(array, min=-limit, max=limit).astype(held_as)


def setup_inputs(seed: int = 0) -> dict:
    seeds = jax.random.split(jax.random.key(seed), 6)
    blocks = noise(seeds[0], (BLOCKS, EDGE, EDGE * EDGE), 1.0, 6.0, ((0, 32),))
    factor_b = noise(seeds[1], (SECOND, RANK), 0.0625, 0.3984375, ((0, 4),))
    factor_c = noise(seeds[2], (THIRD, RANK), 0.0625, 0.3984375, ((0, 8),))
    block_coords = draw_block_coords(jax.random.fold_in(seeds[5], 71), 0)
    block_count = draw_block_count(jax.random.fold_in(seeds[5], 71), 0)
    return {"blocks": blocks, "factor_b": factor_b, "factor_c": factor_c, "block_coords": block_coords, "block_count": block_count}


def reference(blocks, factor_b, factor_c, block_coords, block_count):
    highest = lax.Precision.HIGHEST
    b_blocks = factor_b.reshape(-1, EDGE, RANK)
    c_blocks = factor_c.reshape(-1, EDGE, RANK)
    gram_b = jnp.einsum('jar,jas->jrs', b_blocks.astype(jnp.float32), b_blocks.astype(jnp.float32), precision=highest)
    gram_c = jnp.einsum('kar,kas->krs', c_blocks.astype(jnp.float32), c_blocks.astype(jnp.float32), precision=highest)
    slot_ids = jnp.arange(BLOCKS, dtype=jnp.int32)
    source = slot_ids // SLOTS
    weight = (slot_ids % SLOTS < block_count[source]).astype(jnp.float32)
    first_row = block_coords[:, 0].astype(jnp.int32)
    second_row = (source // N_KA * SECOND_DEV + block_coords[:, 1]).astype(jnp.int32)
    third_row = (source % N_KA * THIRD_DEV + block_coords[:, 2]).astype(jnp.int32)
    first_total = FIRST_DEV * N_JA * N_KA
    moments = jnp.zeros((first_total, EDGE, RANK), jnp.float32)
    grams = jnp.zeros((first_total, RANK, RANK), jnp.float32)

    def step(carry, item):
        moment_sum, gram_sum = carry
        tensor_block, row, second, third, scale = item
        b_rows = lax.dynamic_index_in_dim(b_blocks, second, 0, keepdims=False).astype(jnp.float32)
        c_rows = lax.dynamic_index_in_dim(c_blocks, third, 0, keepdims=False).astype(jnp.float32)
        khatri = (b_rows[:, None, :] * c_rows[None, :, :]).reshape(EDGE * EDGE, RANK).astype(jnp.bfloat16)
        term = jnp.dot(tensor_block.astype(jnp.float32), khatri.astype(jnp.float32), preferred_element_type=jnp.float32).astype(jnp.bfloat16)
        moment_sum = moment_sum.at[row].add(term.astype(jnp.float32) * scale)
        pair = lax.dynamic_index_in_dim(gram_b, second, 0, keepdims=False) * lax.dynamic_index_in_dim(gram_c, third, 0, keepdims=False)
        gram_sum = gram_sum.at[row].add(pair * scale)
        return ((moment_sum, gram_sum), None)
    (moments, grams), unused = lax.scan(step, (moments, grams), (blocks, first_row, second_row, third_row, weight))
    identity = jnp.eye(RANK, dtype=jnp.float32)

    def solve_one(item):
        gram, moment = item
        return jnp.linalg.solve(gram + 0.1 * identity, moment.T).T
    solved = lax.map(solve_one, (grams, moments))
    return solved.reshape(-1, RANK)
```

```python
import functools

import jax
import jax.numpy as jnp
from jax import lax
from jax.experimental import pallas as pl
from jax.experimental.pallas import tpu as pltpu
from jax.sharding import PartitionSpec as P

ALL = ("ja", "ka")
CODE_ROWS = 8
BUFFERS = 4
RIDGE = 0.1
TOLERANCE = 1e-6
FIXED_STEPS = 6
MOST_STEPS = 600
MIB = 1 << 20


def xor_permute(value, mask):
    count = lax.axis_size(ALL)
    return lax.ppermute(value, ALL, [(i, i ^ mask) for i in range(count)])


def stage_plan(size_ja, size_ka):
    low = size_ka.bit_length() - 1
    core = low
    rest = [low + 1 + i for i in range(size_ja.bit_length() - 2)] + list(range(low))
    return [[core]] + [rest[i : i + 2] for i in range(0, len(rest), 2)]


def terms_kernel(
    order, coords, count, me, blocks, b_ref, c_ref, keep_ref, send_ref, buffers, sems
):
    edge = c_ref.shape[1]
    third_dev = c_ref.shape[0]
    half = keep_ref.shape[0]
    live = count[0]
    device = me[0]

    def fetch(slot, place):
        return pltpu.make_async_copy(blocks.at[slot], buffers.at[place], sems.at[place])

    for place in range(BUFFERS):

        @pl.when(place < live)
        def _():
            fetch(place, place).start()

    keep_ref[...] = jnp.zeros_like(keep_ref)
    send_ref[...] = jnp.zeros_like(send_ref)
    lanes = lax.broadcasted_iota(jnp.int32, (CODE_ROWS, c_ref.shape[2]), 1)

    def step(slot, carry):
        place = lax.rem(slot, BUFFERS)
        fetch(slot, place).wait()
        second = coords[slot * 3 + 1]
        third = coords[slot * 3 + 2]
        b_rows = b_ref[second].astype(jnp.float32)
        c_rows = c_ref[third]
        total = jnp.zeros((edge, c_rows.shape[1]), jnp.float32)
        group = 8
        for first in range(0, edge, group):
            pieces = []
            for row in range(first, first + group):
                spread = jnp.broadcast_to(b_rows[row : row + 1], (16, b_rows.shape[1])).astype(jnp.bfloat16)
                for start in range(0, edge, 16):
                    pieces.append(spread * c_rows[start : start + 16])
            khatri = jnp.concatenate(pieces, axis=0)
            part = buffers[place, :, first * edge : (first + group) * edge]
            total += jnp.dot(part, khatri, preferred_element_type=jnp.float32)
        term = total.astype(jnp.bfloat16)
        relative = jnp.bitwise_xor(coords[slot * 3], device)
        target = 0
        for new_bit, old_bit in enumerate(order):
            target += (lax.shift_right_logical(relative, old_bit) & 1) << new_bit
        code = (second * third_dev + third + 1).astype(jnp.float32)
        row_code = jnp.where(lanes == relative, code, 0.0).astype(jnp.bfloat16)

        @pl.when(target < half)
        def _():
            keep_ref[target, :edge] = term
            keep_ref[target, edge:] = row_code

        @pl.when(target >= half)
        def _():
            send_ref[target - half, :edge] = term
            send_ref[target - half, edge:] = row_code

        @pl.when(slot + BUFFERS < live)
        def _():
            fetch(slot + BUFFERS, place).start()

        return carry

    lax.fori_loop(0, live, step, 0)


def own_terms(order, blocks, b_blocks, c_blocks, coords, count, me, total_rows):
    slots, edge, width = blocks.shape
    rank = b_blocks.shape[2]
    half = jax.ShapeDtypeStruct((total_rows // 2, edge + CODE_ROWS, rank), jnp.bfloat16)
    smem = pl.BlockSpec(memory_space=pltpu.SMEM)
    vmem = pl.BlockSpec(memory_space=pltpu.VMEM)
    return pl.pallas_call(
        functools.partial(terms_kernel, order),
        out_shape=(half, half),
        in_specs=[smem, smem, smem, pl.BlockSpec(memory_space=pl.ANY), vmem, vmem],
        out_specs=(vmem, vmem),
        scratch_shapes=[
            pltpu.VMEM((BUFFERS, edge, width), blocks.dtype),
            pltpu.SemaphoreType.DMA((BUFFERS,)),
        ],
        compiler_params=pltpu.CompilerParams(vmem_limit_bytes=20 * MIB),
        cost_estimate=pl.CostEstimate(
            flops=slots * edge * width * rank * 2,
            bytes_accessed=slots * edge * width * 2,
            transcendentals=0,
        ),
        name="own_terms",
    )(coords.reshape(-1), count, me, blocks, b_blocks, c_blocks)


def grams_kernel(*refs):
    gram_ref = refs[-1]
    edge = refs[0].shape[1]
    place = 0
    for ref in refs[:-1]:
        for block in range(ref.shape[0]):
            rows = ref[block]
            gram_ref[place] = lax.dot_general(
                rows, rows, (((0,), (0,)), ((), ())), preferred_element_type=jnp.float32
            )
            place += 1
    del edge


def grams_of(parts):
    rank = parts[0].shape[2]
    edge = parts[0].shape[1]
    number = sum(p.shape[0] for p in parts)
    vmem = pl.BlockSpec(memory_space=pltpu.VMEM)
    return pl.pallas_call(
        grams_kernel,
        out_shape=jax.ShapeDtypeStruct((number, rank, rank), jnp.float32),
        in_specs=[vmem] * len(parts),
        out_specs=vmem,
        compiler_params=pltpu.CompilerParams(vmem_limit_bytes=(number * rank * rank * 4 + 6 * MIB)),
        cost_estimate=pl.CostEstimate(
            flops=number * edge * rank * rank * 2,
            bytes_accessed=number * edge * rank * 2,
            transcendentals=0,
        ),
        name="grams",
    )(*parts)


def solve_kernel(shape, me, moment_ref, gram_b, gram_c, out_ref, system, work):
    size_ja, size_ka, second_dev, third_dev, b_place, c_place = shape
    edge, rank = out_ref.shape
    lanes = lax.broadcasted_iota(jnp.int32, (1, rank), 1)
    code_row = moment_ref[edge : edge + 1, :]
    eye = lax.broadcasted_iota(jnp.int32, (rank, rank), 0) == lax.broadcasted_iota(jnp.int32, (rank, rank), 1)
    system[...] = jnp.where(eye, RIDGE, 0.0)
    core = me[1]
    for source in range(size_ja * size_ka):
        code = jnp.sum(jnp.where(lanes == source, code_row, 0.0)).astype(jnp.int32)

        @pl.when(code > 0)
        def _(source=source, code=code):
            second = lax.div(code - 1, third_dev)
            third = lax.rem(code - 1, third_dev)
            b_index = b_place[source // size_ka] * second_dev + second
            per_half = third_dev // 2
            far = jnp.bitwise_xor(lax.div(third, per_half), core)
            c_index = (far * size_ka + c_place[source % size_ka]) * per_half + lax.rem(third, per_half)
            system[...] += gram_b[b_index] * gram_c[c_index]

    matrix = system[...]
    moment = moment_ref[:edge, :]
    scale = jnp.max(jnp.abs(moment), axis=1, keepdims=True)
    goal = moment / jnp.where(scale > 0, scale, 1.0)
    inverse = 1.0 / jnp.sum(jnp.where(eye, matrix, 0.0), axis=0, keepdims=True)
    limit = TOLERANCE * TOLERANCE * jnp.sum(goal * goal, axis=1, keepdims=True)

    def advance(state):
        x, r, p, rz = state
        q = jnp.dot(p, system[...], precision=lax.Precision.HIGHEST, preferred_element_type=jnp.float32)
        pq = jnp.sum(p * q, axis=1, keepdims=True)
        alpha = jnp.where(pq > 0, rz / jnp.where(pq > 0, pq, 1.0), 0.0)
        x = x + alpha * p
        r = r - alpha * q
        z = r * inverse
        new_rz = jnp.sum(r * z, axis=1, keepdims=True)
        beta = jnp.where(rz > 0, new_rz / jnp.where(rz > 0, rz, 1.0), 0.0)
        return x, r, z + beta * p, new_rz

    def excess(r):
        return jnp.max(jnp.sum(r * r, axis=1, keepdims=True) - limit)

    z = goal * inverse
    state = (jnp.zeros_like(goal), goal, z, jnp.sum(goal * z, axis=1, keepdims=True))
    for _ in range(FIXED_STEPS):
        state = advance(state)

    def unfinished(carry):
        return (carry[0] < MOST_STEPS) & (carry[1] > 0)

    def more(carry):
        following = advance(carry[2])
        return carry[0] + 1, excess(following[1]), following

    _, left, state = lax.while_loop(unfinished, more, (0, excess(state[1]), state))
    out_ref[...] = state[0] * scale

    @pl.when(jnp.logical_not(left <= 0))
    def _():
        work[:rank] = matrix
        work[rank:] = goal

        def sweep(column, carry):
            row = work[pl.ds(column, 1), :]
            pivot = jnp.sum(jnp.where(lanes == column, row, 0.0), axis=1, keepdims=True)
            current = work[...]
            factor = jnp.sum(jnp.where(lanes == column, current, 0.0), axis=1, keepdims=True) / pivot
            work[...] = jnp.where(lanes == column, factor, current - factor * row)
            return carry

        lax.fori_loop(0, rank, sweep, 0)
        out_ref[...] = work[rank:] * scale


def solve(shape, me, moment, gram_b, gram_c, edge):
    rank = moment.shape[-1]
    vmem = pl.BlockSpec(memory_space=pltpu.VMEM)
    return pl.pallas_call(
        functools.partial(solve_kernel, shape),
        out_shape=jax.ShapeDtypeStruct((edge, rank), jnp.float32),
        in_specs=[pl.BlockSpec(memory_space=pltpu.SMEM), vmem, vmem, vmem],
        out_specs=vmem,
        scratch_shapes=[
            pltpu.VMEM((rank, rank), jnp.float32),
            pltpu.VMEM((rank + edge, rank), jnp.float32),
        ],
        compiler_params=pltpu.CompilerParams(
            vmem_limit_bytes=(gram_b.size + gram_c.size) * 4 + 8 * MIB
        ),
        name="solve",
    )(me, moment, gram_b, gram_c)


def body(blocks, factor_b, factor_c, block_coords, block_count):
    edge = blocks.shape[1]
    rank = factor_b.shape[1]
    size_ja, size_ka = lax.axis_size("ja"), lax.axis_size("ka")
    devices = size_ja * size_ka
    second_dev = factor_b.shape[0] // edge
    third_dev = factor_c.shape[0] // edge
    assert devices & (devices - 1) == 0 and size_ja >= 2 and devices <= rank
    assert second_dev * third_dev < 256 and third_dev % 2 == 0
    plan = stage_plan(size_ja, size_ka)
    order = [bit for group in reversed(plan) for bit in group]
    index = lax.axis_index(ALL)
    core = lax.rem(lax.axis_index("ja"), 2)
    me = jnp.stack([index, core]).astype(jnp.int32)
    b_blocks = factor_b.reshape(second_dev, edge, rank)
    c_blocks = factor_c.reshape(third_dev, edge, rank)
    core_mask = size_ka

    b_parts, b_place = [b_blocks], [0] * size_ja
    held = [0]
    for bit in list(range(1, size_ja.bit_length() - 1)) + [0]:
        mask = 1 << bit
        b_parts = b_parts + [xor_permute(part, mask * size_ka) for part in b_parts]
        held = held + [q ^ mask for q in held]
    for place, q in enumerate(held):
        b_place[q] = place
    half_c = lax.dynamic_slice_in_dim(c_blocks, core * (third_dev // 2), third_dev // 2, 0)
    held, c_place = [0], [0] * size_ka
    for bit in reversed(range(size_ka.bit_length() - 1)):
        half_c = jnp.concatenate([half_c, xor_permute(half_c, 1 << bit)], axis=0)
        held = held + [q ^ (1 << bit) for q in held]
    for place, q in enumerate(held):
        c_place[q] = place
    other_c = xor_permute(half_c, core_mask)
    gram_b = grams_of(b_parts)
    gram_c = grams_of([half_c, other_c])

    keep, send = own_terms(order, blocks, b_blocks, c_blocks, block_coords, block_count, me, devices)
    received = xor_permute(send, core_mask)
    total = keep.astype(jnp.float32) + received.astype(jnp.float32)
    for group in plan[1:]:
        pieces = total.reshape((1 << len(group), -1) + total.shape[1:])
        arrived = []
        for piece in range(1, 1 << len(group)):
            mask = sum(1 << bit for i, bit in enumerate(group) if piece >> i & 1)
            arrived.append(xor_permute(pieces[piece].astype(jnp.bfloat16), mask))
        total = pieces[0]
        for part in arrived:
            total = total + part.astype(jnp.float32)
    shape = (size_ja, size_ka, second_dev, third_dev, tuple(b_place), tuple(c_place))
    return solve(shape, me, total[0], gram_b, gram_c, edge)


def solution(mesh):
    placed = (P(ALL, None, None), P("ja", None), P("ka", None), P(ALL, None), P(ALL))
    return jax.shard_map(body, mesh=mesh, in_specs=placed, out_specs=P(ALL, None), check_vma=False)
```

```python
import functools

import jax
import jax.numpy as jnp
from jax import lax
from jax.experimental import pallas as pl
from jax.experimental.pallas import tpu as pltpu
from jax.sharding import PartitionSpec as P

ALL = ("ja", "ka")
CODE_ROWS = 8
AHEAD = 4
GROUP = 8
RIDGE = 0.1
TOLERANCE = 1e-6
FIXED_STEPS = 6
MOST_STEPS = 600
MIB = 1 << 20


def xor_permute(value, mask):
    count = lax.axis_size(ALL)
    return lax.ppermute(value, ALL, [(i, i ^ mask) for i in range(count)])


def stage_plan(size_ja, size_ka):
    low = size_ka.bit_length() - 1
    core = low
    rest = [low + 1 + i for i in range(size_ja.bit_length() - 2)] + list(range(low))
    return [[core]] + [rest[i : i + 2] for i in range(0, len(rest), 2)]


def terms_kernel(
    order,
    coords_hbm,
    count,
    me,
    blocks,
    b_hbm,
    c_hbm,
    keep_ref,
    send_ref,
    held,
    b_ref,
    c_ref,
    sems,
    factor_sems,
    coords,
    waiting,
    first,
    second,
):
    edge, rank = c_ref.shape[1:]
    third_dev = c_ref.shape[0]
    half = keep_ref.shape[0]
    live = count[0]
    device = me[0]

    def fetch(slot):
        return pltpu.make_async_copy(blocks.at[slot], held.at[slot], sems.at[slot])

    factors = [
        pltpu.make_async_copy(source, place, factor_sems.at[index])
        for index, (source, place) in enumerate(((coords_hbm, coords), (b_hbm, b_ref), (c_hbm, c_ref)))
    ]
    for copy in factors:
        copy.start()
    fetch(0).start()

    for cell in range(waiting.shape[0]):
        waiting[cell] = -1
    factors[0].wait()

    def assign(slot, passes):
        cell = coords[1, slot] * third_dev + coords[2, slot]
        opened = waiting[cell]
        joins = opened >= 0
        place = jnp.where(joins, opened, passes)
        first[place] = jnp.where(joins, first[place], slot)
        second[place] = slot
        waiting[cell] = jnp.where(joins, -1, passes)
        return jnp.where(joins, passes, passes + 1)

    passes = lax.fori_loop(0, live, assign, 0)

    def fetch_pass(index):
        one, two = first[index], second[index]

        @pl.when(one > 0)
        def _():
            fetch(one).start()

        @pl.when(one != two)
        def _():
            fetch(two).start()

    for index in range(AHEAD):

        @pl.when(index < passes)
        def _():
            fetch_pass(index)

    keep_ref[...] = jnp.zeros_like(keep_ref)
    send_ref[...] = jnp.zeros_like(send_ref)
    for copy in factors[1:]:
        copy.wait()
    lanes = lax.broadcasted_iota(jnp.int32, (CODE_ROWS, rank), 1)

    def put(slot, code, term):
        relative = jnp.bitwise_xor(coords[0, slot], device)
        target = 0
        for new_bit, old_bit in enumerate(order):
            target += (lax.shift_right_logical(relative, old_bit) & 1) << new_bit
        row_code = jnp.where(lanes == relative, code, 0.0).astype(jnp.bfloat16)

        @pl.when(target < half)
        def _():
            keep_ref[target, :edge] = term
            keep_ref[target, edge:] = row_code

        @pl.when(target >= half)
        def _():
            send_ref[target - half, :edge] = term
            send_ref[target - half, edge:] = row_code

    def step(index, carry):
        @pl.when(index + AHEAD < passes)
        def _():
            fetch_pass(index + AHEAD)

        one, two = first[index], second[index]
        fetch(one).wait()

        @pl.when(one != two)
        def _():
            fetch(two).wait()

        b_index, c_index = coords[1, one], coords[2, one]
        b_rows = b_ref[b_index].astype(jnp.float32)
        c_rows = c_ref[c_index]
        total = jnp.zeros((2 * edge, rank), jnp.float32)
        for start in range(0, edge, GROUP):
            pieces = []
            for row in range(start, start + GROUP):
                spread = jnp.broadcast_to(b_rows[row : row + 1], (16, rank)).astype(jnp.bfloat16)
                for low in range(0, edge, 16):
                    pieces.append(spread * c_rows[low : low + 16])
            khatri = jnp.concatenate(pieces, axis=0)
            columns = slice(start * edge, (start + GROUP) * edge)
            part = jnp.concatenate([held[one, :, columns], held[two, :, columns]], axis=0)
            total += jnp.dot(part, khatri, preferred_element_type=jnp.float32)
        term = total.astype(jnp.bfloat16)
        code = (b_index * third_dev + c_index + 1).astype(jnp.float32)
        put(one, code, term[:edge])
        put(two, code, term[edge:])
        return carry

    lax.fori_loop(0, passes, step, 0)


def own_terms(order, blocks, b_blocks, c_blocks, coords, count, me, total_rows):
    slots, edge, width = blocks.shape
    rank = b_blocks.shape[2]
    half = jax.ShapeDtypeStruct((total_rows // 2, edge + CODE_ROWS, rank), jnp.bfloat16)
    smem = pl.BlockSpec(memory_space=pltpu.SMEM)
    vmem = pl.BlockSpec(memory_space=pltpu.VMEM)
    hbm = pl.BlockSpec(memory_space=pltpu.HBM)
    in_hbm = functools.partial(pltpu.with_memory_space_constraint, memory_space=pltpu.HBM)
    return pl.pallas_call(
        functools.partial(terms_kernel, order),
        out_shape=(half, half),
        in_specs=[hbm, smem, smem, hbm, hbm, hbm],
        out_specs=(vmem, vmem),
        scratch_shapes=[
            pltpu.VMEM((slots, edge, width), blocks.dtype),
            pltpu.VMEM(b_blocks.shape, b_blocks.dtype),
            pltpu.VMEM(c_blocks.shape, c_blocks.dtype),
            pltpu.SemaphoreType.DMA((slots,)),
            pltpu.SemaphoreType.DMA((3,)),
            pltpu.SMEM((3, slots), jnp.int32),
            pltpu.SMEM((b_blocks.shape[0] * c_blocks.shape[0],), jnp.int32),
            pltpu.SMEM((slots,), jnp.int32),
            pltpu.SMEM((slots,), jnp.int32),
        ],
        compiler_params=pltpu.CompilerParams(vmem_limit_bytes=52 * MIB),
        cost_estimate=pl.CostEstimate(
            flops=slots * edge * width * rank * 2,
            bytes_accessed=slots * edge * width * 2,
            transcendentals=0,
        ),
        name="own_terms",
    )(in_hbm(coords.T), count, me, blocks, in_hbm(b_blocks), in_hbm(c_blocks))


def grams_kernel(*refs):
    gram_ref = refs[-1]
    edge = refs[0].shape[1]
    place = 0
    for ref in refs[:-1]:
        for block in range(ref.shape[0]):
            rows = ref[block]
            gram_ref[place] = lax.dot_general(
                rows, rows, (((0,), (0,)), ((), ())), preferred_element_type=jnp.float32
            )
            place += 1
    del edge


def grams_of(parts):
    rank = parts[0].shape[2]
    edge = parts[0].shape[1]
    number = sum(p.shape[0] for p in parts)
    vmem = pl.BlockSpec(memory_space=pltpu.VMEM)
    return pl.pallas_call(
        grams_kernel,
        out_shape=jax.ShapeDtypeStruct((number, rank, rank), jnp.float32),
        in_specs=[vmem] * len(parts),
        out_specs=vmem,
        compiler_params=pltpu.CompilerParams(vmem_limit_bytes=(number * rank * rank * 4 + 6 * MIB)),
        cost_estimate=pl.CostEstimate(
            flops=number * edge * rank * rank * 2,
            bytes_accessed=number * edge * rank * 2,
            transcendentals=0,
        ),
        name="grams",
    )(*parts)


def split3(value):
    high = value.astype(jnp.bfloat16)
    rest = value - high.astype(jnp.float32)
    middle = rest.astype(jnp.bfloat16)
    return high, middle, (rest - middle.astype(jnp.float32)).astype(jnp.bfloat16)


def solve_kernel(shape, me, moment_ref, gram_b, gram_c, out_ref, system, parts, work, b_list, c_list):
    size_ja, size_ka, second_dev, third_dev, b_place, c_place = shape
    edge, rank = out_ref.shape
    sources = size_ja * size_ka
    lanes = lax.broadcasted_iota(jnp.int32, (1, rank), 1)
    core = me[1]

    width = (second_dev * third_dev).bit_length()
    per = 24 // width
    weight = jnp.left_shift(1, width * lax.rem(lanes, per)).astype(jnp.float32)
    weighted = moment_ref[edge : edge + 1, :] * weight
    packed = [
        jnp.sum(jnp.where(lax.div(lanes, per) == group, weighted, 0.0)).astype(jnp.int32)
        for group in range(pl.cdiv(sources, per))
    ]
    half = third_dev // 2
    live = 0
    for source in range(sources):
        code = lax.shift_right_logical(packed[source // per], width * (source % per)) & ((1 << width) - 1)
        cell = jnp.maximum(code - 1, 0)
        second, third = lax.div(cell, third_dev), lax.rem(cell, third_dev)
        far = jnp.bitwise_xor(lax.div(third, half), core)
        b_list[live] = b_place[source // size_ka] * second_dev + second
        c_list[live] = (far * size_ka + c_place[source % size_ka]) * half + lax.rem(third, half)
        live = live + (code > 0).astype(jnp.int32)

    strip = min(64, rank)
    for low in range(0, rank, strip):
        rows = lax.broadcasted_iota(jnp.int32, (strip, rank), 0) + low
        columns = lax.broadcasted_iota(jnp.int32, (strip, rank), 1)

        def add(index, total, low=low):
            left = gram_b[b_list[index], low : low + strip, :]
            return total + left * gram_c[c_list[index], low : low + strip, :]

        total = lax.fori_loop(0, live, add, jnp.where(rows == columns, RIDGE, 0.0))
        system[low : low + strip] = total
        for place, part in enumerate(split3(total)):
            parts[place, low : low + strip] = part

    eye = lax.broadcasted_iota(jnp.int32, (rank, rank), 0) == lax.broadcasted_iota(jnp.int32, (rank, rank), 1)
    inverse = 1.0 / jnp.sum(jnp.where(eye, system[...], 0.0), axis=0, keepdims=True)
    moment = moment_ref[:edge, :]
    scale = jnp.max(jnp.abs(moment), axis=1, keepdims=True)
    goal = moment / jnp.where(scale > 0, scale, 1.0)
    limit = TOLERANCE * TOLERANCE * jnp.sum(goal * goal, axis=1, keepdims=True)

    def times_system(value):
        high, middle, low = split3(value)
        three = jnp.dot(
            jnp.concatenate([high, middle, low], axis=0), parts[0], preferred_element_type=jnp.float32
        )
        two = jnp.dot(jnp.concatenate([high, middle], axis=0), parts[1], preferred_element_type=jnp.float32)
        one = jnp.dot(high, parts[2], preferred_element_type=jnp.float32)
        small = (one + two[edge:]) + three[2 * edge :]
        return three[:edge] + ((two[:edge] + three[edge : 2 * edge]) + small)

    def advance(state):
        x, r, p, rz = state
        q = times_system(p)
        pq = jnp.sum(p * q, axis=1, keepdims=True)
        alpha = jnp.where(pq > 0, rz / jnp.where(pq > 0, pq, 1.0), 0.0)
        x = x + alpha * p
        r = r - alpha * q
        z = r * inverse
        new_rz = jnp.sum(r * z, axis=1, keepdims=True)
        beta = jnp.where(rz > 0, new_rz / jnp.where(rz > 0, rz, 1.0), 0.0)
        return x, r, z + beta * p, new_rz

    def excess(r):
        return jnp.max(jnp.sum(r * r, axis=1, keepdims=True) - limit)

    z = goal * inverse
    state = (jnp.zeros_like(goal), goal, z, jnp.sum(goal * z, axis=1, keepdims=True))
    for _ in range(FIXED_STEPS):
        state = advance(state)

    def unfinished(carry):
        return (carry[0] < MOST_STEPS) & (carry[1] > 0)

    def more(carry):
        following = advance(carry[2])
        return carry[0] + 1, excess(following[1]), following

    _, left, state = lax.while_loop(unfinished, more, (0, excess(state[1]), state))
    out_ref[...] = state[0] * scale

    @pl.when(jnp.logical_not(left <= 0))
    def _():
        work[:rank] = system[...]
        work[rank:] = goal

        def sweep(column, carry):
            row = work[pl.ds(column, 1), :]
            pivot = jnp.sum(jnp.where(lanes == column, row, 0.0), axis=1, keepdims=True)
            current = work[...]
            factor = jnp.sum(jnp.where(lanes == column, current, 0.0), axis=1, keepdims=True) / pivot
            work[...] = jnp.where(lanes == column, factor, current - factor * row)
            return carry

        lax.fori_loop(0, rank, sweep, 0)
        out_ref[...] = work[rank:] * scale


def solve(shape, me, moment, gram_b, gram_c, edge):
    rank = moment.shape[-1]
    sources = shape[0] * shape[1]
    vmem = pl.BlockSpec(memory_space=pltpu.VMEM)
    return pl.pallas_call(
        functools.partial(solve_kernel, shape),
        out_shape=jax.ShapeDtypeStruct((edge, rank), jnp.float32),
        in_specs=[pl.BlockSpec(memory_space=pltpu.SMEM), vmem, vmem, vmem],
        out_specs=vmem,
        scratch_shapes=[
            pltpu.VMEM((rank, rank), jnp.float32),
            pltpu.VMEM((3, rank, rank), jnp.bfloat16),
            pltpu.VMEM((rank + edge, rank), jnp.float32),
            pltpu.SMEM((sources + 1,), jnp.int32),
            pltpu.SMEM((sources + 1,), jnp.int32),
        ],
        compiler_params=pltpu.CompilerParams(
            vmem_limit_bytes=(gram_b.size + gram_c.size) * 4 + 8 * MIB
        ),
        name="solve",
    )(me, moment, gram_b, gram_c)


def body(blocks, factor_b, factor_c, block_coords, block_count):
    edge = blocks.shape[1]
    rank = factor_b.shape[1]
    size_ja, size_ka = lax.axis_size("ja"), lax.axis_size("ka")
    devices = size_ja * size_ka
    second_dev = factor_b.shape[0] // edge
    third_dev = factor_c.shape[0] // edge
    assert devices & (devices - 1) == 0 and size_ja >= 2 and devices <= rank
    assert second_dev * third_dev < 256 and third_dev % 2 == 0
    plan = stage_plan(size_ja, size_ka)
    order = [bit for group in reversed(plan) for bit in group]
    index = lax.axis_index(ALL)
    core = lax.rem(lax.axis_index("ja"), 2)
    me = jnp.stack([index, core]).astype(jnp.int32)
    b_blocks = factor_b.reshape(second_dev, edge, rank)
    c_blocks = factor_c.reshape(third_dev, edge, rank)
    core_mask = size_ka

    b_parts, b_place, held = [b_blocks], [0] * size_ja, [0]
    for bit in list(range(1, size_ja.bit_length() - 1)) + [0]:
        b_parts = b_parts + [xor_permute(part, size_ka << bit) for part in b_parts]
        held = held + [q ^ (1 << bit) for q in held]
    for place, q in enumerate(held):
        b_place[q] = place
    c_half = lax.dynamic_slice_in_dim(c_blocks, core * (third_dev // 2), third_dev // 2, 0)
    c_place, held = [0] * size_ka, [0]
    for bit in [0] + list(reversed(range(1, size_ka.bit_length() - 1))):
        c_half = jnp.concatenate([c_half, xor_permute(c_half, 1 << bit)], axis=0)
        held = held + [q ^ (1 << bit) for q in held]
    for place, q in enumerate(held):
        c_place[q] = place
    c_other = xor_permute(c_half, core_mask)
    gram_b = grams_of(b_parts)
    gram_c = grams_of([c_half, c_other])

    keep, send = own_terms(order, blocks, b_blocks, c_blocks, block_coords, block_count, me, devices)
    received = xor_permute(send, core_mask)
    total = keep.astype(jnp.float32) + received.astype(jnp.float32)
    for group in plan[1:]:
        pieces = total.reshape((1 << len(group), -1) + total.shape[1:])
        total = pieces[0]
        arrived = []
        for piece in range(1, 1 << len(group)):
            mask = sum(1 << bit for i, bit in enumerate(group) if piece >> i & 1)
            arrived.append(xor_permute(pieces[piece].astype(jnp.bfloat16), mask))
        for part in arrived:
            total = total + part.astype(jnp.float32)
    shape = (size_ja, size_ka, second_dev, third_dev, tuple(b_place), tuple(c_place))
    return solve(shape, me, total[0], gram_b, gram_c, edge)


def solution(mesh):
    placed = (P(ALL, None, None), P("ja", None), P("ka", None), P(ALL, None), P(ALL))
    return jax.shard_map(body, mesh=mesh, in_specs=placed, out_specs=P(ALL, None), check_vma=False)
```

```python
import functools

import jax
import jax.numpy as jnp
from jax import lax
from jax.experimental import pallas as pl
from jax.experimental.pallas import tpu as pltpu
from jax.sharding import PartitionSpec as P

ALL = ("ja", "ka")
CODE_ROWS = 8
AHEAD = 4
GROUP = 8
STRIP = 128
RIDGE = 0.1
TOLERANCE = 1e-6
FIXED_STEPS = 6
MOST_STEPS = 600
MIB = 1 << 20


def xor_permute(value, mask):
    count = lax.axis_size(ALL)
    return lax.ppermute(value, ALL, [(i, i ^ mask) for i in range(count)])


def stage_plan(size_ja, size_ka):
    low = size_ka.bit_length() - 1
    core = low
    rest = [low + 1 + i for i in range(size_ja.bit_length() - 2)] + list(range(low))
    return [[core]] + [rest[i : i + 2] for i in range(0, len(rest), 2)]


def terms_kernel(
    order,
    coords_hbm,
    count_hbm,
    blocks,
    b_hbm,
    c_hbm,
    keep_ref,
    send_ref,
    held,
    b_ref,
    c_ref,
    sems,
    factor_sems,
    coords,
    count,
    waiting,
    first,
    second,
):
    edge, rank = c_ref.shape[1:]
    third_dev = c_ref.shape[0]
    low_bits = (third_dev - 1).bit_length()
    half = keep_ref.shape[0]
    device = lax.axis_index(ALL)

    def fetch(slot):
        return pltpu.make_async_copy(blocks.at[slot], held.at[slot], sems.at[slot])

    copies = [
        pltpu.make_async_copy(source, place, factor_sems.at[index])
        for index, (source, place) in enumerate(
            ((coords_hbm, coords), (count_hbm, count), (b_hbm, b_ref), (c_hbm, c_ref))
        )
    ]
    for copy in copies:
        copy.start()
    fetch(0).start()

    for cell in range(waiting.shape[0]):
        waiting[cell] = -1
    copies[0].wait()
    copies[1].wait()
    live = count[0]

    def assign(slot, passes):
        cell = coords[1, slot] * third_dev + coords[2, slot]
        opened = waiting[cell]
        joins = opened >= 0
        place = jnp.where(joins, opened, passes)
        first[place] = jnp.where(joins, first[place], slot)
        second[place] = slot
        waiting[cell] = jnp.where(joins, -1, passes)
        return jnp.where(joins, passes, passes + 1)

    passes = lax.fori_loop(0, live, assign, 0)

    def fetch_pass(index):
        one, two = first[index], second[index]

        @pl.when(one > 0)
        def _():
            fetch(one).start()

        @pl.when(one != two)
        def _():
            fetch(two).start()

    for index in range(AHEAD):

        @pl.when(index < passes)
        def _():
            fetch_pass(index)

    keep_ref[...] = jnp.zeros_like(keep_ref)
    send_ref[...] = jnp.zeros_like(send_ref)
    for copy in copies[2:]:
        copy.wait()
    lanes = lax.broadcasted_iota(jnp.int32, (CODE_ROWS, rank), 1)

    def put(slot, code, term):
        relative = jnp.bitwise_xor(coords[0, slot], device)
        target = 0
        for new_bit, old_bit in enumerate(order):
            target += (lax.shift_right_logical(relative, old_bit) & 1) << new_bit
        row_code = jnp.where(lanes == relative, code, 0.0).astype(jnp.bfloat16)

        @pl.when(target < half)
        def _():
            keep_ref[target, :edge] = term
            keep_ref[target, edge:] = row_code

        @pl.when(target >= half)
        def _():
            send_ref[target - half, :edge] = term
            send_ref[target - half, edge:] = row_code

    def step(index, carry):
        @pl.when(index + AHEAD < passes)
        def _():
            fetch_pass(index + AHEAD)

        one, two = first[index], second[index]
        fetch(one).wait()

        @pl.when(one != two)
        def _():
            fetch(two).wait()

        b_index, c_index = coords[1, one], coords[2, one]
        b_rows = b_ref[b_index].astype(jnp.float32)
        c_rows = c_ref[c_index]
        total = jnp.zeros((2 * edge, rank), jnp.float32)
        for start in range(0, edge, GROUP):
            pieces = []
            for row in range(start, start + GROUP):
                spread = jnp.broadcast_to(b_rows[row : row + 1], (16, rank)).astype(jnp.bfloat16)
                for low in range(0, edge, 16):
                    pieces.append(spread * c_rows[low : low + 16])
            khatri = jnp.concatenate(pieces, axis=0)
            columns = slice(start * edge, (start + GROUP) * edge)
            part = jnp.concatenate([held[one, :, columns], held[two, :, columns]], axis=0)
            total += jnp.dot(part, khatri, preferred_element_type=jnp.float32)
        term = total.astype(jnp.bfloat16)
        code = ((b_index << low_bits | c_index) << 1 | 1).astype(jnp.float32)
        put(one, code, term[:edge])
        put(two, code, term[edge:])
        return carry

    lax.fori_loop(0, passes, step, 0)


def own_terms(order, blocks, b_blocks, c_blocks, coords, count, total_rows):
    slots, edge, width = blocks.shape
    rank = b_blocks.shape[2]
    half = jax.ShapeDtypeStruct((total_rows // 2, edge + CODE_ROWS, rank), jnp.bfloat16)
    vmem = pl.BlockSpec(memory_space=pltpu.VMEM)
    hbm = pl.BlockSpec(memory_space=pltpu.HBM)
    in_hbm = functools.partial(pltpu.with_memory_space_constraint, memory_space=pltpu.HBM)
    return pl.pallas_call(
        functools.partial(terms_kernel, order),
        out_shape=(half, half),
        in_specs=[hbm, pl.BlockSpec(memory_space=pl.ANY), hbm, hbm, hbm],
        out_specs=(vmem, vmem),
        scratch_shapes=[
            pltpu.VMEM((slots, edge, width), blocks.dtype),
            pltpu.VMEM(b_blocks.shape, b_blocks.dtype),
            pltpu.VMEM(c_blocks.shape, c_blocks.dtype),
            pltpu.SemaphoreType.DMA((slots,)),
            pltpu.SemaphoreType.DMA((4,)),
            pltpu.SMEM((3, slots), jnp.int32),
            pltpu.SMEM((1,), jnp.int32),
            pltpu.SMEM((b_blocks.shape[0] * c_blocks.shape[0],), jnp.int32),
            pltpu.SMEM((slots,), jnp.int32),
            pltpu.SMEM((slots,), jnp.int32),
        ],
        compiler_params=pltpu.CompilerParams(vmem_limit_bytes=52 * MIB),
        cost_estimate=pl.CostEstimate(
            flops=slots * edge * width * rank * 2,
            bytes_accessed=slots * edge * width * 2,
            transcendentals=0,
        ),
        name="own_terms",
    )(in_hbm(coords.T), count, *(in_hbm(operand) for operand in (blocks, b_blocks, c_blocks)))


def grams_kernel(*refs):
    gram_ref = refs[-1]
    edge = refs[0].shape[1]
    place = 0
    for ref in refs[:-1]:
        for block in range(ref.shape[0]):
            rows = ref[block]
            gram_ref[place] = lax.dot_general(
                rows, rows, (((0,), (0,)), ((), ())), preferred_element_type=jnp.float32
            )
            place += 1
    del edge


def grams_of(parts):
    rank = parts[0].shape[2]
    edge = parts[0].shape[1]
    number = sum(p.shape[0] for p in parts)
    vmem = pl.BlockSpec(memory_space=pltpu.VMEM)
    return pl.pallas_call(
        grams_kernel,
        out_shape=jax.ShapeDtypeStruct((number, rank, rank), jnp.float32),
        in_specs=[vmem] * len(parts),
        out_specs=vmem,
        compiler_params=pltpu.CompilerParams(vmem_limit_bytes=(number * rank * rank * 4 + 6 * MIB)),
        cost_estimate=pl.CostEstimate(
            flops=number * edge * rank * rank * 2,
            bytes_accessed=number * edge * rank * 2,
            transcendentals=0,
        ),
        name="grams",
    )(*parts)


def split3(value):
    high = value.astype(jnp.bfloat16)
    rest = value - high.astype(jnp.float32)
    middle = rest.astype(jnp.bfloat16)
    return high, middle, (rest - middle.astype(jnp.float32)).astype(jnp.bfloat16)


def solve_kernel(shape, moment_ref, gram_b, gram_c, out_ref, system, parts, work, b_list, c_list):
    size_ja, size_ka, second_dev, third_dev, b_place, c_place = shape
    edge, rank = out_ref.shape
    sources = size_ja * size_ka
    lanes = lax.broadcasted_iota(jnp.int32, (1, rank), 1)
    core = lax.axis_index("ja") & 1

    low_bits = (third_dev - 1).bit_length()
    width = low_bits + (second_dev - 1).bit_length() + 1
    per = 24 // width
    weight = jnp.left_shift(1, width * lax.rem(lanes, per)).astype(jnp.float32)
    weighted = moment_ref[edge : edge + 1, :] * weight
    packed = [
        jnp.sum(jnp.where(lax.div(lanes, per) == group, weighted, 0.0)).astype(jnp.int32)
        for group in range(pl.cdiv(sources, per))
    ]
    half = third_dev // 2
    live = 0
    for source in range(sources):
        code = lax.shift_right_logical(packed[source // per], width * (source % per)) & ((1 << width) - 1)
        field = lax.shift_right_logical(code, 1)
        second, third = lax.shift_right_logical(field, low_bits), field & ((1 << low_bits) - 1)
        upper = (third >= half).astype(jnp.int32)
        far = jnp.bitwise_xor(upper, core)
        b_list[live] = b_place[source // size_ka] * second_dev + second
        c_list[live] = (far * size_ka + c_place[source % size_ka]) * half + third - upper * half
        live = live + (code & 1)

    strip = min(STRIP, rank)
    for low in range(0, rank, strip):
        rows = lax.broadcasted_iota(jnp.int32, (strip, rank), 0) + low
        columns = lax.broadcasted_iota(jnp.int32, (strip, rank), 1)

        def add(index, total, low=low):
            left = gram_b[b_list[index], low : low + strip, :]
            return total + left * gram_c[c_list[index], low : low + strip, :]

        total = lax.fori_loop(0, live, add, jnp.where(rows == columns, RIDGE, 0.0))
        system[low : low + strip] = total
        for place, part in enumerate(split3(total)):
            parts[place, low : low + strip] = part

    eye = lax.broadcasted_iota(jnp.int32, (rank, rank), 0) == lax.broadcasted_iota(jnp.int32, (rank, rank), 1)
    inverse = 1.0 / jnp.sum(jnp.where(eye, system[...], 0.0), axis=0, keepdims=True)
    moment = moment_ref[:edge, :]
    scale = jnp.max(jnp.abs(moment), axis=1, keepdims=True)
    goal = moment / jnp.where(scale > 0, scale, 1.0)
    limit = TOLERANCE * TOLERANCE * jnp.sum(goal * goal, axis=1, keepdims=True)

    def times_system(value):
        high, middle, low = split3(value)
        three = jnp.dot(
            jnp.concatenate([high, middle, low], axis=0), parts[0], preferred_element_type=jnp.float32
        )
        two = jnp.dot(jnp.concatenate([high, middle], axis=0), parts[1], preferred_element_type=jnp.float32)
        one = jnp.dot(high, parts[2], preferred_element_type=jnp.float32)
        small = (one + two[edge:]) + three[2 * edge :]
        return three[:edge] + ((two[:edge] + three[edge : 2 * edge]) + small)

    def advance(state):
        x, r, p, rz = state
        q = times_system(p)
        pq = jnp.sum(p * q, axis=1, keepdims=True)
        alpha = jnp.where(pq > 0, rz / jnp.where(pq > 0, pq, 1.0), 0.0)
        x = x + alpha * p
        r = r - alpha * q
        z = r * inverse
        new_rz = jnp.sum(r * z, axis=1, keepdims=True)
        beta = jnp.where(rz > 0, new_rz / jnp.where(rz > 0, rz, 1.0), 0.0)
        return x, r, z + beta * p, new_rz

    def excess(r):
        return jnp.max(jnp.sum(r * r, axis=1, keepdims=True) - limit)

    z = goal * inverse
    state = (jnp.zeros_like(goal), goal, z, jnp.sum(goal * z, axis=1, keepdims=True))
    for _ in range(FIXED_STEPS):
        state = advance(state)

    def unfinished(carry):
        return (carry[0] < MOST_STEPS) & (carry[1] > 0)

    def more(carry):
        following = advance(carry[2])
        return carry[0] + 1, excess(following[1]), following

    _, left, state = lax.while_loop(unfinished, more, (0, excess(state[1]), state))
    out_ref[...] = state[0] * scale

    @pl.when(jnp.logical_not(left <= 0))
    def _():
        work[:rank] = system[...]
        work[rank:] = goal

        def sweep(column, carry):
            row = work[pl.ds(column, 1), :]
            pivot = jnp.sum(jnp.where(lanes == column, row, 0.0), axis=1, keepdims=True)
            current = work[...]
            factor = jnp.sum(jnp.where(lanes == column, current, 0.0), axis=1, keepdims=True) / pivot
            work[...] = jnp.where(lanes == column, factor, current - factor * row)
            return carry

        lax.fori_loop(0, rank, sweep, 0)
        out_ref[...] = work[rank:] * scale


def solve(shape, moment, gram_b, gram_c, edge):
    rank = moment.shape[-1]
    sources = shape[0] * shape[1]
    vmem = pl.BlockSpec(memory_space=pltpu.VMEM)
    return pl.pallas_call(
        functools.partial(solve_kernel, shape),
        out_shape=jax.ShapeDtypeStruct((edge, rank), jnp.float32),
        in_specs=[vmem, vmem, vmem],
        out_specs=vmem,
        scratch_shapes=[
            pltpu.VMEM((rank, rank), jnp.float32),
            pltpu.VMEM((3, rank, rank), jnp.bfloat16),
            pltpu.VMEM((rank + edge, rank), jnp.float32),
            pltpu.SMEM((sources + 1,), jnp.int32),
            pltpu.SMEM((sources + 1,), jnp.int32),
        ],
        compiler_params=pltpu.CompilerParams(
            vmem_limit_bytes=(gram_b.size + gram_c.size) * 4 + 8 * MIB
        ),
        name="solve",
    )(moment, gram_b, gram_c)


def body(blocks, factor_b, factor_c, block_coords, block_count):
    edge = blocks.shape[1]
    rank = factor_b.shape[1]
    size_ja, size_ka = lax.axis_size("ja"), lax.axis_size("ka")
    devices = size_ja * size_ka
    second_dev = factor_b.shape[0] // edge
    third_dev = factor_c.shape[0] // edge
    assert devices & (devices - 1) == 0 and size_ja >= 2 and devices <= rank
    assert second_dev * third_dev <= 64 and third_dev % 2 == 0
    plan = stage_plan(size_ja, size_ka)
    order = [bit for group in reversed(plan) for bit in group]
    core = lax.axis_index("ja") & 1
    b_blocks = factor_b.reshape(second_dev, edge, rank)
    c_blocks = factor_c.reshape(third_dev, edge, rank)
    core_mask = size_ka

    b_parts, b_place, held = [b_blocks], [0] * size_ja, [0]
    for bit in list(range(1, size_ja.bit_length() - 1)) + [0]:
        b_parts = b_parts + [xor_permute(part, size_ka << bit) for part in b_parts]
        held = held + [q ^ (1 << bit) for q in held]
    for place, q in enumerate(held):
        b_place[q] = place
    c_half = lax.dynamic_slice_in_dim(c_blocks, core * (third_dev // 2), third_dev // 2, 0)
    c_place, held = [0] * size_ka, [0]
    top = size_ka.bit_length() - 2
    for group in [[0]] + [[bit] for bit in range(top, 0, -1)]:
        masks = [sum(1 << bit for i, bit in enumerate(group) if piece >> i & 1) for piece in range(1 << len(group))]
        arrived = [c_half]
        for piece, mask in enumerate(masks[1:], 1):
            arrived.append(xor_permute(c_half, mask))
        c_half = jnp.concatenate(arrived, axis=0)
        held = [q ^ mask for mask in masks for q in held]
    for place, q in enumerate(held):
        c_place[q] = place
    c_other = xor_permute(c_half, core_mask)
    gram_b = grams_of(b_parts)
    gram_c = grams_of([c_half, c_other])

    keep, send = own_terms(order, blocks, b_blocks, c_blocks, block_coords, block_count, devices)
    received = xor_permute(send, core_mask)
    total = keep.astype(jnp.float32) + received.astype(jnp.float32)
    for group in plan[1:]:
        pieces = total.reshape((1 << len(group), -1) + total.shape[1:])
        total = pieces[0]
        arrived = []
        for piece in range(1, 1 << len(group)):
            mask = sum(1 << bit for i, bit in enumerate(group) if piece >> i & 1)
            arrived.append(xor_permute(pieces[piece].astype(jnp.bfloat16), mask))
        for part in arrived:
            total = total + part.astype(jnp.float32)
    shape = (size_ja, size_ka, second_dev, third_dev, tuple(b_place), tuple(c_place))
    return solve(shape, total[0], gram_b, gram_c, edge)


def solution(mesh):
    placed = (P(ALL, None, None), P("ja", None), P("ka", None), P(ALL, None), P(ALL))
    return jax.shard_map(body, mesh=mesh, in_specs=placed, out_specs=P(ALL, None), check_vma=False)
```

```python
import functools

import jax
import jax.numpy as jnp
from jax import lax
from jax.experimental import pallas as pl
from jax.experimental.pallas import tpu as pltpu
from jax.sharding import PartitionSpec as P

ALL = ("ja", "ka")
CODE_ROWS = 8
AHEAD = 4
GROUP = 8
STRIP = 128
RIDGE = 0.1
TOLERANCE = 1e-6
FIXED_STEPS = 6
MOST_STEPS = 600
MIB = 1 << 20


def xor_permute(value, mask):
    count = lax.axis_size(ALL)
    return lax.ppermute(value, ALL, [(i, i ^ mask) for i in range(count)])


def padded(rows):
    return -(-rows // CODE_ROWS) * CODE_ROWS


def stage_plan(size_ja, size_ka):
    low = size_ka.bit_length() - 1
    core = low
    rest = [low + 1 + i for i in range(size_ja.bit_length() - 2)] + list(range(low))
    return [[core]] + [rest[i : i + 2] for i in range(0, len(rest), 2)]


def terms_kernel(
    order,
    coords_hbm,
    count_hbm,
    blocks,
    b_hbm,
    c_hbm,
    keep_ref,
    send_ref,
    held,
    b_ref,
    c_ref,
    sems,
    factor_sems,
    coords,
    count,
    codes,
    waiting,
    first,
    second,
):
    edge, rank = c_ref.shape[1:]
    third_dev = c_ref.shape[0]
    low_bits = (third_dev - 1).bit_length()
    half = codes.shape[0] // 2
    device = lax.axis_index(ALL)

    def fetch(slot):
        return pltpu.make_async_copy(blocks.at[slot], held.at[slot], sems.at[slot])

    copies = [
        pltpu.make_async_copy(source, place, factor_sems.at[index])
        for index, (source, place) in enumerate(
            ((coords_hbm, coords), (count_hbm, count), (b_hbm, b_ref), (c_hbm, c_ref))
        )
    ]
    for copy in copies:
        copy.start()
    fetch(0).start()

    keep_ref[...] = jnp.zeros_like(keep_ref)
    send_ref[...] = jnp.zeros_like(send_ref)
    codes[...] = jnp.zeros_like(codes)
    for cell in range(waiting.shape[0]):
        waiting[cell] = -1
    copies[0].wait()
    copies[1].wait()
    live = count[0]

    def assign(slot, passes):
        cell = coords[1, slot] * third_dev + coords[2, slot]
        opened = waiting[cell]
        joins = opened >= 0
        place = jnp.where(joins, opened, passes)
        first[place] = jnp.where(joins, first[place], slot)
        second[place] = slot
        waiting[cell] = jnp.where(joins, -1, passes)
        return jnp.where(joins, passes, passes + 1)

    passes = lax.fori_loop(0, live, assign, 0)

    def fetch_pass(index):
        one, two = first[index], second[index]

        @pl.when(one > 0)
        def _():
            fetch(one).start()

        @pl.when(one != two)
        def _():
            fetch(two).start()

    for index in range(AHEAD):

        @pl.when(index < passes)
        def _():
            fetch_pass(index)

    for copy in copies[2:]:
        copy.wait()
    lanes = lax.broadcasted_iota(jnp.int32, (1, rank), 1)

    def put(slot, code, term):
        relative = jnp.bitwise_xor(coords[0, slot], device)
        target = 0
        for new_bit, old_bit in enumerate(order):
            target += (lax.shift_right_logical(relative, old_bit) & 1) << new_bit
        codes[pl.ds(target, 1), :] = jnp.where(lanes == relative, code, 0.0)

        @pl.when(target < half)
        def _():
            keep_ref[pl.ds(pl.multiple_of(target * edge, edge), edge), :] = term

        @pl.when(target >= half)
        def _():
            send_ref[pl.ds(pl.multiple_of((target - half) * edge, edge), edge), :] = term

    def step(index, carry):
        @pl.when(index + AHEAD < passes)
        def _():
            fetch_pass(index + AHEAD)

        one, two = first[index], second[index]
        fetch(one).wait()

        @pl.when(one != two)
        def _():
            fetch(two).wait()

        b_index, c_index = coords[1, one], coords[2, one]
        b_rows = b_ref[b_index].astype(jnp.float32)
        c_rows = c_ref[c_index]
        total = jnp.zeros((2 * edge, rank), jnp.float32)
        for start in range(0, edge, GROUP):
            pieces = []
            for row in range(start, start + GROUP):
                spread = jnp.broadcast_to(b_rows[row : row + 1], (16, rank)).astype(jnp.bfloat16)
                for low in range(0, edge, 16):
                    pieces.append(spread * c_rows[low : low + 16])
            khatri = jnp.concatenate(pieces, axis=0)
            columns = slice(start * edge, (start + GROUP) * edge)
            part = jnp.concatenate([held[one, :, columns], held[two, :, columns]], axis=0)
            total += jnp.dot(part, khatri, preferred_element_type=jnp.float32)
        term = total.astype(jnp.bfloat16)
        code = ((b_index << low_bits | c_index) << 1 | 1).astype(jnp.float32)
        put(one, code, term[:edge])
        put(two, code, term[edge:])
        return carry

    lax.fori_loop(0, passes, step, 0)
    keep_ref[half * edge : half * edge + half, :] = codes[:half].astype(jnp.bfloat16)
    send_ref[half * edge : half * edge + half, :] = codes[half:].astype(jnp.bfloat16)


def own_terms(order, blocks, b_blocks, c_blocks, coords, count, total_rows):
    slots, edge, width = blocks.shape
    rank = b_blocks.shape[2]
    half = jax.ShapeDtypeStruct((total_rows // 2 * edge + padded(total_rows // 2), rank), jnp.bfloat16)
    vmem = pl.BlockSpec(memory_space=pltpu.VMEM)
    hbm = pl.BlockSpec(memory_space=pltpu.HBM)
    in_hbm = functools.partial(pltpu.with_memory_space_constraint, memory_space=pltpu.HBM)
    return pl.pallas_call(
        functools.partial(terms_kernel, order),
        out_shape=(half, half),
        in_specs=[hbm, pl.BlockSpec(memory_space=pl.ANY), hbm, hbm, hbm],
        out_specs=(vmem, vmem),
        scratch_shapes=[
            pltpu.VMEM((slots, edge, width), blocks.dtype),
            pltpu.VMEM(b_blocks.shape, b_blocks.dtype),
            pltpu.VMEM(c_blocks.shape, c_blocks.dtype),
            pltpu.SemaphoreType.DMA((slots,)),
            pltpu.SemaphoreType.DMA((4,)),
            pltpu.SMEM((3, slots), jnp.int32),
            pltpu.SMEM((1,), jnp.int32),
            pltpu.VMEM((total_rows, rank), jnp.float32),
            pltpu.SMEM((b_blocks.shape[0] * c_blocks.shape[0],), jnp.int32),
            pltpu.SMEM((slots,), jnp.int32),
            pltpu.SMEM((slots,), jnp.int32),
        ],
        compiler_params=pltpu.CompilerParams(vmem_limit_bytes=52 * MIB),
        cost_estimate=pl.CostEstimate(
            flops=slots * edge * width * rank * 2,
            bytes_accessed=slots * edge * width * 2,
            transcendentals=0,
        ),
        name="own_terms",
    )(in_hbm(coords.T), count, *(in_hbm(operand) for operand in (blocks, b_blocks, c_blocks)))


def grams_kernel(*refs):
    gram_ref = refs[-1]
    edge = refs[0].shape[1]
    place = 0
    for ref in refs[:-1]:
        for block in range(ref.shape[0]):
            rows = ref[block]
            gram_ref[place] = lax.dot_general(
                rows, rows, (((0,), (0,)), ((), ())), preferred_element_type=jnp.float32
            )
            place += 1
    del edge


def grams_of(parts):
    rank = parts[0].shape[2]
    edge = parts[0].shape[1]
    number = sum(p.shape[0] for p in parts)
    vmem = pl.BlockSpec(memory_space=pltpu.VMEM)
    return pl.pallas_call(
        grams_kernel,
        out_shape=jax.ShapeDtypeStruct((number, rank, rank), jnp.float32),
        in_specs=[vmem] * len(parts),
        out_specs=vmem,
        compiler_params=pltpu.CompilerParams(vmem_limit_bytes=(number * rank * rank * 4 + 6 * MIB)),
        cost_estimate=pl.CostEstimate(
            flops=number * edge * rank * rank * 2,
            bytes_accessed=number * edge * rank * 2,
            transcendentals=0,
        ),
        name="grams",
    )(*parts)


def split3(value):
    high = value.astype(jnp.bfloat16)
    rest = value - high.astype(jnp.float32)
    middle = rest.astype(jnp.bfloat16)
    return high, middle, (rest - middle.astype(jnp.float32)).astype(jnp.bfloat16)


def solve_kernel(shape, moment_ref, gram_b, early_c, late_c, out_ref, system, parts, work, b_list, c_list):
    size_ja, size_ka, second_dev, third_dev, b_place, c_place, last = shape
    edge, rank = out_ref.shape
    sources = size_ja * size_ka
    lanes = lax.broadcasted_iota(jnp.int32, (1, rank), 1)
    core = lax.axis_index("ja") & 1

    low_bits = (third_dev - 1).bit_length()
    width = low_bits + (second_dev - 1).bit_length() + 1
    per = 24 // width
    weight = jnp.left_shift(1, width * lax.rem(lanes, per)).astype(jnp.float32)
    weighted = moment_ref[edge : edge + 1, :] * weight
    packed = [
        jnp.sum(jnp.where(lax.div(lanes, per) == group, weighted, 0.0)).astype(jnp.int32)
        for group in range(pl.cdiv(sources, per))
    ]
    half = third_dev // 2
    live = [0, 0]
    for source in range(sources):
        number, offset = c_place[source % size_ka]
        late = int(number == last)
        code = lax.shift_right_logical(packed[source // per], width * (source % per)) & ((1 << width) - 1)
        field = lax.shift_right_logical(code, 1)
        second, third = lax.shift_right_logical(field, low_bits), field & ((1 << low_bits) - 1)
        upper = (third >= half).astype(jnp.int32)
        far = jnp.bitwise_xor(upper, core)
        block = (0 if late else number) * 2 * third_dev + (far * 2 + offset) * half + third - upper * half
        b_list[late, live[late]] = b_place[source // size_ka] * second_dev + second
        c_list[late, live[late]] = block
        live[late] = live[late] + (code & 1)

    strip = min(STRIP, rank)
    for low in range(0, rank, strip):
        rows = lax.broadcasted_iota(jnp.int32, (strip, rank), 0) + low
        columns = lax.broadcasted_iota(jnp.int32, (strip, rank), 1)

        total = jnp.where(rows == columns, RIDGE, 0.0)
        for late, gram_c in enumerate((early_c, late_c)):

            def add(index, total, late=late, gram_c=gram_c, low=low):
                left = gram_b[b_list[late, index], low : low + strip, :]
                return total + left * gram_c[c_list[late, index], low : low + strip, :]

            total = lax.fori_loop(0, live[late], add, total)
        system[low : low + strip] = total
        for place, part in enumerate(split3(total)):
            parts[place, low : low + strip] = part

    eye = lax.broadcasted_iota(jnp.int32, (rank, rank), 0) == lax.broadcasted_iota(jnp.int32, (rank, rank), 1)
    inverse = 1.0 / jnp.sum(jnp.where(eye, system[...], 0.0), axis=0, keepdims=True)
    moment = moment_ref[:edge, :]
    scale = jnp.max(jnp.abs(moment), axis=1, keepdims=True)
    goal = moment / jnp.where(scale > 0, scale, 1.0)
    limit = TOLERANCE * TOLERANCE * jnp.sum(goal * goal, axis=1, keepdims=True)

    def times_system(value):
        high, middle, low = split3(value)
        three = jnp.dot(
            jnp.concatenate([high, middle, low], axis=0), parts[0], preferred_element_type=jnp.float32
        )
        two = jnp.dot(jnp.concatenate([high, middle], axis=0), parts[1], preferred_element_type=jnp.float32)
        one = jnp.dot(high, parts[2], preferred_element_type=jnp.float32)
        small = (one + two[edge:]) + three[2 * edge :]
        return three[:edge] + ((two[:edge] + three[edge : 2 * edge]) + small)

    def advance(state):
        x, r, p, rz = state
        q = times_system(p)
        pq = jnp.sum(p * q, axis=1, keepdims=True)
        alpha = jnp.where(pq > 0, rz / jnp.where(pq > 0, pq, 1.0), 0.0)
        x = x + alpha * p
        r = r - alpha * q
        z = r * inverse
        new_rz = jnp.sum(r * z, axis=1, keepdims=True)
        beta = jnp.where(rz > 0, new_rz / jnp.where(rz > 0, rz, 1.0), 0.0)
        return x, r, z + beta * p, new_rz

    def excess(r):
        return jnp.max(jnp.sum(r * r, axis=1, keepdims=True) - limit)

    z = goal * inverse
    state = (jnp.zeros_like(goal), goal, z, jnp.sum(goal * z, axis=1, keepdims=True))
    for _ in range(FIXED_STEPS):
        state = advance(state)

    def unfinished(carry):
        return (carry[0] < MOST_STEPS) & (carry[1] > 0)

    def more(carry):
        following = advance(carry[2])
        return carry[0] + 1, excess(following[1]), following

    _, left, state = lax.while_loop(unfinished, more, (0, excess(state[1]), state))
    out_ref[...] = state[0] * scale

    @pl.when(jnp.logical_not(left <= 0))
    def _():
        work[:rank] = system[...]
        work[rank:] = goal

        def sweep(column, carry):
            row = work[pl.ds(column, 1), :]
            pivot = jnp.sum(jnp.where(lanes == column, row, 0.0), axis=1, keepdims=True)
            current = work[...]
            factor = jnp.sum(jnp.where(lanes == column, current, 0.0), axis=1, keepdims=True) / pivot
            work[...] = jnp.where(lanes == column, factor, current - factor * row)
            return carry

        lax.fori_loop(0, rank, sweep, 0)
        out_ref[...] = work[rank:] * scale


def solve(shape, moment, gram_b, gram_c, edge):
    rank = moment.shape[-1]
    sources = shape[0] * shape[1]
    vmem = pl.BlockSpec(memory_space=pltpu.VMEM)
    return pl.pallas_call(
        functools.partial(solve_kernel, shape),
        out_shape=jax.ShapeDtypeStruct((edge, rank), jnp.float32),
        in_specs=[vmem] * 4,
        out_specs=vmem,
        scratch_shapes=[
            pltpu.VMEM((rank, rank), jnp.float32),
            pltpu.VMEM((3, rank, rank), jnp.bfloat16),
            pltpu.VMEM((rank + edge, rank), jnp.float32),
            pltpu.SMEM((2, sources + 1), jnp.int32),
            pltpu.SMEM((2, sources + 1), jnp.int32),
        ],
        compiler_params=pltpu.CompilerParams(
            vmem_limit_bytes=(gram_b.size + sum(c.size for c in gram_c)) * 4 + 8 * MIB
        ),
        name="solve",
    )(moment, gram_b, *gram_c)


def body(blocks, factor_b, factor_c, block_coords, block_count):
    edge = blocks.shape[1]
    rank = factor_b.shape[1]
    size_ja, size_ka = lax.axis_size("ja"), lax.axis_size("ka")
    devices = size_ja * size_ka
    second_dev = factor_b.shape[0] // edge
    third_dev = factor_c.shape[0] // edge
    assert devices & (devices - 1) == 0 and size_ja >= 2 and devices <= rank
    assert second_dev * third_dev <= 64 and third_dev % 2 == 0
    plan = stage_plan(size_ja, size_ka)
    order = [bit for group in reversed(plan) for bit in group]
    core = lax.axis_index("ja") & 1
    b_blocks = factor_b.reshape(second_dev, edge, rank)
    c_blocks = factor_c.reshape(third_dev, edge, rank)
    core_mask = size_ka

    b_parts, b_place, held = [b_blocks], [0] * size_ja, [0]
    for bit in list(range(1, size_ja.bit_length() - 1)) + [0]:
        b_parts = b_parts + [xor_permute(part, size_ka << bit) for part in b_parts]
        held = held + [q ^ (1 << bit) for q in held]
    for place, q in enumerate(held):
        b_place[q] = place
    c_place = [0] * size_ka
    c_near = xor_permute(c_blocks, 1)
    halves = [lax.dynamic_slice_in_dim(c, core * (third_dev // 2), third_dev // 2, 0) for c in (c_blocks, c_near)]
    c_sets = [jnp.concatenate(halves, axis=0)]
    starts = [0]
    for bit in range(size_ka.bit_length() - 2, 0, -1):
        for number in range(len(c_sets)):
            c_sets.append(xor_permute(c_sets[number], 1 << bit))
        starts = starts + [q ^ (1 << bit) for q in starts]
    for number, q in enumerate(starts):
        c_place[q], c_place[q ^ 1] = (number, 0), (number, 1)
    c_other = []
    for number, part in enumerate(c_sets):
        c_other.append(xor_permute(part, core_mask))
    gram_b = grams_of(b_parts)
    c_pairs = [[part, other] for part, other in zip(c_sets, c_other)]
    gram_c = [grams_of(sum(c_pairs[:-1], []))]
    gram_c.append(grams_of(c_pairs[-1]))

    keep, send = own_terms(order, blocks, b_blocks, c_blocks, block_coords, block_count, devices)
    received = xor_permute(send, core_mask)
    total = keep.astype(jnp.float32) + received.astype(jnp.float32)
    rows = devices // 2
    for group in plan[1:]:
        rows >>= len(group)
        number = 1 << len(group)
        terms = [total[rows * edge * piece : rows * edge * (piece + 1)] for piece in range(number)]
        first_code = rows * number * edge
        codes = [total[first_code + rows * piece : first_code + rows * (piece + 1)] for piece in range(number)]
        spare = ((0, padded(rows) - rows), (0, 0))
        messages = [jnp.concatenate([part, jnp.pad(code, spare)], axis=0) for part, code in zip(terms, codes)]
        arrived = []
        for piece in range(1, number):
            mask = sum(1 << bit for i, bit in enumerate(group) if piece >> i & 1)
            arrived.append(xor_permute(messages[piece].astype(jnp.bfloat16), mask))
        total = messages[0]
        for part in arrived:
            total = total + part.astype(jnp.float32)
    shape = (size_ja, size_ka, second_dev, third_dev, tuple(b_place), tuple(c_place), len(c_sets) - 1)
    return solve(shape, total, gram_b, gram_c, edge)


def solution(mesh):
    placed = (P(ALL, None, None), P("ja", None), P("ka", None), P(ALL, None), P(ALL))
    return jax.shard_map(body, mesh=mesh, in_specs=placed, out_specs=P(ALL, None), check_vma=False)
```

```python
import functools

import jax
import jax.numpy as jnp
from jax import lax
from jax.experimental import pallas as pl
from jax.experimental.pallas import tpu as pltpu
from jax.sharding import PartitionSpec as P

ALL = ("ja", "ka")
CODE_ROWS = 8
AHEAD = 8
GROUP = 16
TOGETHER = 4
STRIP = 128
RIDGE = 0.1
TOLERANCE = 5e-6
FIXED_STEPS = 5
MOST_STEPS = 600
MIB = 1 << 20


def xor_permute(value, mask):
    count = lax.axis_size(ALL)
    return lax.ppermute(value, ALL, [(i, i ^ mask) for i in range(count)])


def padded(rows):
    return -(-rows // CODE_ROWS) * CODE_ROWS


def stage_plan(size_ja, size_ka):
    low = size_ka.bit_length() - 1
    core = low
    rest = [low + 1 + i for i in range(size_ja.bit_length() - 2)] + list(range(low))
    return [[core]] + [rest[i : i + 2] for i in range(0, len(rest), 2)]


def terms_kernel(
    order,
    coords_hbm,
    count_hbm,
    blocks,
    b_hbm,
    c_hbm,
    keep_ref,
    send_ref,
    held,
    b_ref,
    c_ref,
    sems,
    factor_sems,
    coords,
    count,
    codes,
    waiting,
    first,
    second,
):
    edge, rank = c_ref.shape[1:]
    third_dev = c_ref.shape[0]
    low_bits = (third_dev - 1).bit_length()
    half = codes.shape[0] // 2
    device = lax.axis_index(ALL)

    def fetch(slot):
        return pltpu.make_async_copy(blocks.at[slot], held.at[slot], sems.at[slot])

    copies = [
        pltpu.make_async_copy(source, place, factor_sems.at[index])
        for index, (source, place) in enumerate(
            ((coords_hbm, coords), (count_hbm, count), (b_hbm, b_ref), (c_hbm, c_ref))
        )
    ]
    for copy in copies:
        copy.start()
    fetch(0).start()

    keep_ref[...] = jnp.zeros_like(keep_ref)
    send_ref[...] = jnp.zeros_like(send_ref)
    codes[...] = jnp.zeros_like(codes)
    for cell in range(waiting.shape[0]):
        waiting[cell] = -1
    copies[0].wait()
    copies[1].wait()
    live = count[0]

    def assign(slot, passes):
        cell = coords[1, slot] * third_dev + coords[2, slot]
        opened = waiting[cell]
        joins = opened >= 0
        place = jnp.where(joins, opened, passes)
        first[place] = jnp.where(joins, first[place], slot)
        second[place] = slot
        waiting[cell] = jnp.where(joins, -1, passes)
        return jnp.where(joins, passes, passes + 1)

    passes = lax.fori_loop(0, live, assign, 0)

    def fetch_pass(index):
        one, two = first[index], second[index]

        @pl.when(one > 0)
        def _():
            fetch(one).start()

        @pl.when(one != two)
        def _():
            fetch(two).start()

    for index in range(AHEAD):

        @pl.when(index < passes)
        def _():
            fetch_pass(index)

    for copy in copies[2:]:
        copy.wait()
    lanes = lax.broadcasted_iota(jnp.int32, (1, rank), 1)

    def put(slot, code, term):
        relative = jnp.bitwise_xor(coords[0, slot], device)
        target = 0
        for new_bit, old_bit in enumerate(order):
            target += (lax.shift_right_logical(relative, old_bit) & 1) << new_bit
        codes[pl.ds(target, 1), :] = jnp.where(lanes == relative, code, 0.0)

        @pl.when(target < half)
        def _():
            keep_ref[pl.ds(pl.multiple_of(target * edge, edge), edge), :] = term

        @pl.when(target >= half)
        def _():
            send_ref[pl.ds(pl.multiple_of((target - half) * edge, edge), edge), :] = term

    def multiply(index):
        one, two = first[index], second[index]
        b_index, c_index = coords[1, one], coords[2, one]
        b_rows = b_ref[b_index].astype(jnp.float32)
        c_rows = c_ref[c_index]
        total = jnp.zeros((2 * edge, rank), jnp.float32)
        for start in range(0, edge, GROUP):
            pieces = []
            for row in range(start, start + GROUP):
                spread = jnp.broadcast_to(b_rows[row : row + 1], (16, rank)).astype(jnp.bfloat16)
                for low in range(0, edge, 16):
                    pieces.append(spread * c_rows[low : low + 16])
            khatri = jnp.concatenate(pieces, axis=0)
            columns = slice(start * edge, (start + GROUP) * edge)
            part = jnp.concatenate([held[one, :, columns], held[two, :, columns]], axis=0)
            total += jnp.dot(part, khatri, preferred_element_type=jnp.float32)
        return total.astype(jnp.bfloat16)

    def finish(index, term):
        one, two = first[index], second[index]
        code = ((coords[1, one] << low_bits | coords[2, one]) << 1 | 1).astype(jnp.float32)
        put(one, code, term[:edge])
        put(two, code, term[edge:])

    def await_pass(index):
        one, two = first[index], second[index]

        @pl.when(index + AHEAD < passes)
        def _():
            fetch_pass(index + AHEAD)

        fetch(one).wait()

        @pl.when(one != two)
        def _():
            fetch(two).wait()

    def step(trip, carry):
        indices = [trip * TOGETHER + i for i in range(TOGETHER)]
        for index in indices:
            await_pass(index)
        for index, term in [(index, multiply(index)) for index in indices]:
            finish(index, term)
        return carry

    def rest(index, carry):
        await_pass(index)
        finish(index, multiply(index))
        return carry

    trips = lax.div(passes, TOGETHER)
    lax.fori_loop(0, trips, step, 0)
    lax.fori_loop(trips * TOGETHER, passes, rest, 0)
    keep_ref[half * edge : half * edge + half, :] = codes[:half].astype(jnp.bfloat16)
    send_ref[half * edge : half * edge + half, :] = codes[half:].astype(jnp.bfloat16)


def own_terms(order, blocks, b_blocks, c_blocks, coords, count, total_rows):
    slots, edge, width = blocks.shape
    rank = b_blocks.shape[2]
    half = jax.ShapeDtypeStruct((total_rows // 2 * edge + padded(total_rows // 2), rank), jnp.bfloat16)
    vmem = pl.BlockSpec(memory_space=pltpu.VMEM)
    hbm = pl.BlockSpec(memory_space=pltpu.HBM)
    in_hbm = functools.partial(pltpu.with_memory_space_constraint, memory_space=pltpu.HBM)
    return pl.pallas_call(
        functools.partial(terms_kernel, order),
        out_shape=(half, half),
        in_specs=[hbm, pl.BlockSpec(memory_space=pl.ANY), hbm, hbm, hbm],
        out_specs=(vmem, vmem),
        scratch_shapes=[
            pltpu.VMEM((slots, edge, width), blocks.dtype),
            pltpu.VMEM(b_blocks.shape, b_blocks.dtype),
            pltpu.VMEM(c_blocks.shape, c_blocks.dtype),
            pltpu.SemaphoreType.DMA((slots,)),
            pltpu.SemaphoreType.DMA((4,)),
            pltpu.SMEM((3, slots), jnp.int32),
            pltpu.SMEM((1,), jnp.int32),
            pltpu.VMEM((total_rows, rank), jnp.float32),
            pltpu.SMEM((b_blocks.shape[0] * c_blocks.shape[0],), jnp.int32),
            pltpu.SMEM((slots,), jnp.int32),
            pltpu.SMEM((slots,), jnp.int32),
        ],
        compiler_params=pltpu.CompilerParams(vmem_limit_bytes=52 * MIB),
        cost_estimate=pl.CostEstimate(
            flops=slots * edge * width * rank * 2,
            bytes_accessed=slots * edge * width * 2,
            transcendentals=0,
        ),
        name="own_terms",
    )(in_hbm(coords.T), count, *(in_hbm(operand) for operand in (blocks, b_blocks, c_blocks)))


def grams_kernel(*refs):
    gram_ref = refs[-1]
    edge = refs[0].shape[1]
    place = 0
    for ref in refs[:-1]:
        for block in range(ref.shape[0]):
            rows = ref[block]
            gram_ref[place] = lax.dot_general(
                rows, rows, (((0,), (0,)), ((), ())), preferred_element_type=jnp.float32
            )
            place += 1
    del edge


def grams_of(parts):
    rank = parts[0].shape[2]
    edge = parts[0].shape[1]
    number = sum(p.shape[0] for p in parts)
    vmem = pl.BlockSpec(memory_space=pltpu.VMEM)
    return pl.pallas_call(
        grams_kernel,
        out_shape=jax.ShapeDtypeStruct((number, rank, rank), jnp.float32),
        in_specs=[vmem] * len(parts),
        out_specs=vmem,
        compiler_params=pltpu.CompilerParams(vmem_limit_bytes=(number * rank * rank * 4 + 6 * MIB)),
        cost_estimate=pl.CostEstimate(
            flops=number * edge * rank * rank * 2,
            bytes_accessed=number * edge * rank * 2,
            transcendentals=0,
        ),
        name="grams",
    )(*parts)


def split3(value):
    high = value.astype(jnp.bfloat16)
    rest = value - high.astype(jnp.float32)
    middle = rest.astype(jnp.bfloat16)
    return high, middle, (rest - middle.astype(jnp.float32)).astype(jnp.bfloat16)


def solve_kernel(shape, moment_ref, gram_b, early_c, late_c, out_ref, system, parts, work, b_list, c_list, remaining):
    size_ja, size_ka, second_dev, third_dev, b_place, c_place, last = shape
    edge, rank = out_ref.shape
    sources = size_ja * size_ka
    lanes = lax.broadcasted_iota(jnp.int32, (1, rank), 1)
    core = lax.axis_index("ja") & 1

    low_bits = (third_dev - 1).bit_length()
    width = low_bits + (second_dev - 1).bit_length() + 1
    per = 24 // width
    weight = jnp.left_shift(1, width * lax.rem(lanes, per)).astype(jnp.float32)
    weighted = moment_ref[edge : edge + 1, :] * weight
    packed = [
        jnp.sum(jnp.where(lax.div(lanes, per) == group, weighted, 0.0)).astype(jnp.int32)
        for group in range(pl.cdiv(sources, per))
    ]
    half = third_dev // 2
    live = [0, 0]
    for source in range(sources):
        number, offset = c_place[source % size_ka]
        late = int(number == last)
        code = lax.shift_right_logical(packed[source // per], width * (source % per)) & ((1 << width) - 1)
        field = lax.shift_right_logical(code, 1)
        second, third = lax.shift_right_logical(field, low_bits), field & ((1 << low_bits) - 1)
        upper = (third >= half).astype(jnp.int32)
        far = jnp.bitwise_xor(upper, core)
        block = (0 if late else number) * 2 * third_dev + (far * 2 + offset) * half + third - upper * half
        b_list[late, live[late]] = b_place[source // size_ka] * second_dev + second
        c_list[late, live[late]] = block
        live[late] = live[late] + (code & 1)

    strip = min(STRIP, rank)
    for low in range(0, rank, strip):
        rows = lax.broadcasted_iota(jnp.int32, (strip, rank), 0) + low
        columns = lax.broadcasted_iota(jnp.int32, (strip, rank), 1)

        total = jnp.where(rows == columns, RIDGE, 0.0)
        for late, gram_c in enumerate((early_c, late_c)):

            def product(index, late=late, gram_c=gram_c, low=low):
                left = gram_b[b_list[late, index], low : low + strip, :]
                return left * gram_c[c_list[late, index], low : low + strip, :]

            def add_two(trip, total, product=product):
                return total + product(2 * trip) + product(2 * trip + 1)

            def add(index, total, product=product):
                return total + product(index)

            paired = lax.shift_right_logical(live[late], 1)
            total = lax.fori_loop(0, paired, add_two, total)
            total = lax.fori_loop(2 * paired, live[late], add, total)
        system[low : low + strip] = total
        for place, part in enumerate(split3(total)):
            parts[place, low : low + strip] = part

    eye = lax.broadcasted_iota(jnp.int32, (rank, rank), 0) == lax.broadcasted_iota(jnp.int32, (rank, rank), 1)
    inverse = 1.0 / jnp.sum(jnp.where(eye, system[...], 0.0), axis=0, keepdims=True)
    moment = moment_ref[:edge, :]
    remaining[0] = 0
    scale = jnp.max(jnp.abs(moment), axis=1, keepdims=True)
    goal = moment / jnp.where(scale > 0, scale, 1.0)
    limit = TOLERANCE * TOLERANCE * jnp.sum(goal * goal, axis=1, keepdims=True)

    def times_system(value):
        high, middle, low = split3(value)
        three = jnp.dot(
            jnp.concatenate([high, middle, low], axis=0), parts[0], preferred_element_type=jnp.float32
        )
        two = jnp.dot(jnp.concatenate([high, middle], axis=0), parts[1], preferred_element_type=jnp.float32)
        one = jnp.dot(high, parts[2], preferred_element_type=jnp.float32)
        small = (one + two[edge:]) + three[2 * edge :]
        return three[:edge] + ((two[:edge] + three[edge : 2 * edge]) + small)

    def row_sum(value):
        return jnp.sum(value, axis=1, keepdims=True)

    def ratio(over, under):
        return jnp.where(under > 0, over / jnp.where(under > 0, under, 1.0), 0.0)

    def excess(r):
        return jnp.max(row_sum(r * r) - limit)

    x, r, p, s = jnp.zeros_like(goal), goal, jnp.zeros_like(goal), jnp.zeros_like(goal)
    old_gamma = alpha = None
    for _ in range(FIXED_STEPS):
        z = r * inverse
        q = times_system(z)
        gamma, delta = row_sum(r * z), row_sum(q * z)
        if alpha is None:
            p, s, curvature = z, q, delta
        else:
            beta = ratio(gamma, old_gamma)
            p, s = z + beta * p, q + beta * s
            curvature = delta - beta * ratio(gamma, alpha)
        old_gamma, alpha = gamma, ratio(gamma, curvature)
        x, r = x + alpha * p, r - alpha * s
    out_ref[...] = x * scale

    @pl.when(jnp.logical_not(excess(r) <= 0))
    def _():
        def advance(state):
            x, r, p, rz = state
            q = times_system(p)
            alpha = ratio(rz, row_sum(p * q))
            x, r = x + alpha * p, r - alpha * q
            z = r * inverse
            new_rz = row_sum(r * z)
            return x, r, z + ratio(new_rz, rz) * p, new_rz

        def unfinished(carry):
            return (carry[0] < MOST_STEPS) & (carry[1] > 0)

        def more(carry):
            following = advance(carry[2])
            return carry[0] + 1, excess(following[1]), following

        r = goal - times_system(x)
        z = r * inverse
        _, left, state = lax.while_loop(unfinished, more, (0, excess(r), (x, r, z, row_sum(r * z))))
        out_ref[...] = state[0] * scale
        remaining[0] = jnp.where(left <= 0, 0, 1)

    @pl.when(remaining[0] > 0)
    def _():
        work[:rank] = system[...]
        work[rank:] = goal

        def sweep(column, carry):
            row = work[pl.ds(column, 1), :]
            pivot = jnp.sum(jnp.where(lanes == column, row, 0.0), axis=1, keepdims=True)
            current = work[...]
            factor = jnp.sum(jnp.where(lanes == column, current, 0.0), axis=1, keepdims=True) / pivot
            work[...] = jnp.where(lanes == column, factor, current - factor * row)
            return carry

        lax.fori_loop(0, rank, sweep, 0)
        out_ref[...] = work[rank:] * scale


def solve(shape, moment, gram_b, gram_c, edge):
    rank = moment.shape[-1]
    sources = shape[0] * shape[1]
    vmem = pl.BlockSpec(memory_space=pltpu.VMEM)
    return pl.pallas_call(
        functools.partial(solve_kernel, shape),
        out_shape=jax.ShapeDtypeStruct((edge, rank), jnp.float32),
        in_specs=[vmem] * 4,
        out_specs=vmem,
        scratch_shapes=[
            pltpu.VMEM((rank, rank), jnp.float32),
            pltpu.VMEM((3, rank, rank), jnp.bfloat16),
            pltpu.VMEM((rank + edge, rank), jnp.float32),
            pltpu.SMEM((2, sources + 1), jnp.int32),
            pltpu.SMEM((2, sources + 1), jnp.int32),
            pltpu.SMEM((1,), jnp.int32),
        ],
        compiler_params=pltpu.CompilerParams(
            vmem_limit_bytes=(gram_b.size + sum(c.size for c in gram_c)) * 4 + 8 * MIB
        ),
        name="solve",
    )(moment, gram_b, *gram_c)


def body(blocks, factor_b, factor_c, block_coords, block_count):
    edge = blocks.shape[1]
    rank = factor_b.shape[1]
    size_ja, size_ka = lax.axis_size("ja"), lax.axis_size("ka")
    devices = size_ja * size_ka
    second_dev = factor_b.shape[0] // edge
    third_dev = factor_c.shape[0] // edge
    assert devices & (devices - 1) == 0 and size_ja >= 2 and devices <= rank
    assert second_dev * third_dev <= 64 and third_dev % 2 == 0
    plan = stage_plan(size_ja, size_ka)
    order = [bit for group in reversed(plan) for bit in group]
    core = lax.axis_index("ja") & 1
    b_blocks = factor_b.reshape(second_dev, edge, rank)
    c_blocks = factor_c.reshape(third_dev, edge, rank)
    core_mask = size_ka

    b_parts, b_place, held = [b_blocks], [0] * size_ja, [0]
    for bit in list(range(1, size_ja.bit_length() - 1)) + [0]:
        b_parts = b_parts + [xor_permute(part, size_ka << bit) for part in b_parts]
        held = held + [q ^ (1 << bit) for q in held]
    for place, q in enumerate(held):
        b_place[q] = place
    c_place = [0] * size_ka
    c_near = xor_permute(c_blocks, 1)
    halves = [lax.dynamic_slice_in_dim(c, core * (third_dev // 2), third_dev // 2, 0) for c in (c_blocks, c_near)]
    c_sets = [jnp.concatenate(halves, axis=0)]
    starts = [0]
    for bit in range(size_ka.bit_length() - 2, 0, -1):
        for number in range(len(c_sets)):
            c_sets.append(xor_permute(c_sets[number], 1 << bit))
        starts = starts + [q ^ (1 << bit) for q in starts]
    for number, q in enumerate(starts):
        c_place[q], c_place[q ^ 1] = (number, 0), (number, 1)
    c_other = []
    for number, part in enumerate(c_sets):
        c_other.append(xor_permute(part, core_mask))
    gram_b = grams_of(b_parts)
    c_pairs = [[part, other] for part, other in zip(c_sets, c_other)]
    gram_c = [grams_of(sum(c_pairs[:-1], []))]
    gram_c.append(grams_of(c_pairs[-1]))

    keep, send = own_terms(order, blocks, b_blocks, c_blocks, block_coords, block_count, devices)
    received = xor_permute(send, core_mask)
    total = keep.astype(jnp.float32) + received.astype(jnp.float32)
    rows = devices // 2
    for group in plan[1:]:
        rows >>= len(group)
        number = 1 << len(group)
        terms = [total[rows * edge * piece : rows * edge * (piece + 1)] for piece in range(number)]
        first_code = rows * number * edge
        codes = [total[first_code + rows * piece : first_code + rows * (piece + 1)] for piece in range(number)]
        spare = ((0, padded(rows) - rows), (0, 0))
        messages = [jnp.concatenate([part, jnp.pad(code, spare)], axis=0) for part, code in zip(terms, codes)]
        arrived = []
        for piece in range(1, number):
            mask = sum(1 << bit for i, bit in enumerate(group) if piece >> i & 1)
            arrived.append(xor_permute(messages[piece].astype(jnp.bfloat16), mask))
        total = messages[0]
        for part in arrived:
            total = total + part.astype(jnp.float32)
    shape = (size_ja, size_ka, second_dev, third_dev, tuple(b_place), tuple(c_place), len(c_sets) - 1)
    return solve(shape, total, gram_b, gram_c, edge)


def solution(mesh):
    placed = (P(ALL, None, None), P("ja", None), P("ka", None), P(ALL, None), P(ALL))
    return jax.shard_map(body, mesh=mesh, in_specs=placed, out_specs=P(ALL, None), check_vma=False)
```

```python
import functools

import jax
import jax.numpy as jnp
from jax import lax
from jax.experimental import pallas as pl
from jax.experimental.pallas import tpu as pltpu
from jax.sharding import PartitionSpec as P

ALL = ("ja", "ka")
CODE_ROWS = 8
AHEAD = 8
GROUP = 16
TOGETHER = (3, 2, 1)
STRIP = 128
RIDGE = 0.1
TOLERANCE = 5e-6
FIXED_STEPS = 5
MOST_STEPS = 600
MIB = 1 << 20


def xor_permute(value, mask):
    count = lax.axis_size(ALL)
    return lax.ppermute(value, ALL, [(i, i ^ mask) for i in range(count)])


def padded(rows):
    return -(-rows // CODE_ROWS) * CODE_ROWS


def stage_plan(size_ja, size_ka):
    low = size_ka.bit_length() - 1
    core = low
    rest = [low + 1 + i for i in range(size_ja.bit_length() - 2)] + list(range(low))
    return [[core]] + [rest[i : i + 2] for i in range(0, len(rest), 2)]


def terms_kernel(
    order,
    coords_hbm,
    count_hbm,
    blocks,
    b_hbm,
    c_hbm,
    keep_ref,
    send_ref,
    held,
    b_ref,
    c_ref,
    sems,
    factor_sems,
    coords,
    count,
    codes,
    waiting,
    first,
    second,
):
    edge, rank = c_ref.shape[1:]
    third_dev = c_ref.shape[0]
    low_bits = (third_dev - 1).bit_length()
    half = codes.shape[0] // 2
    device = lax.axis_index(ALL)

    def fetch(slot):
        return pltpu.make_async_copy(blocks.at[slot], held.at[slot], sems.at[slot])

    copies = [
        pltpu.make_async_copy(source, place, factor_sems.at[index])
        for index, (source, place) in enumerate(
            ((coords_hbm, coords), (count_hbm, count), (b_hbm, b_ref), (c_hbm, c_ref))
        )
    ]
    for copy in copies:
        copy.start()
    fetch(0).start()

    keep_ref[...] = jnp.zeros_like(keep_ref)
    send_ref[...] = jnp.zeros_like(send_ref)
    codes[...] = jnp.zeros_like(codes)
    for cell in range(waiting.shape[0]):
        waiting[cell] = -1
    copies[0].wait()
    copies[1].wait()
    live = count[0]

    passes = 0
    spare = held.shape[0]
    for slot in range(spare):
        valid = slot < live
        cell = coords[1, slot] * third_dev + coords[2, slot]
        opened = waiting[cell]
        joins = valid & (opened >= 0)
        opens = valid & (opened < 0)
        first[jnp.where(opens, passes, spare)] = slot
        second[jnp.where(joins, opened, jnp.where(opens, passes, spare))] = slot
        waiting[cell] = jnp.where(opens, passes, jnp.where(joins, -1, opened))
        passes = passes + opens.astype(jnp.int32)

    def fetch_pass(index):
        one, two = first[index], second[index]

        @pl.when(one > 0)
        def _():
            fetch(one).start()

        @pl.when(one != two)
        def _():
            fetch(two).start()

    for index in range(AHEAD):

        @pl.when(index < passes)
        def _():
            fetch_pass(index)

    for copy in copies[2:]:
        copy.wait()
    lanes = lax.broadcasted_iota(jnp.int32, (1, rank), 1)

    def put(slot, code, term):
        relative = jnp.bitwise_xor(coords[0, slot], device)
        target = 0
        for new_bit, old_bit in enumerate(order):
            target += (lax.shift_right_logical(relative, old_bit) & 1) << new_bit
        codes[pl.ds(target, 1), :] = jnp.where(lanes == relative, code, 0.0)

        @pl.when(target < half)
        def _():
            keep_ref[pl.ds(pl.multiple_of(target * edge, edge), edge), :] = term

        @pl.when(target >= half)
        def _():
            send_ref[pl.ds(pl.multiple_of((target - half) * edge, edge), edge), :] = term

    def multiply(index):
        one, two = first[index], second[index]
        b_index, c_index = coords[1, one], coords[2, one]
        b_rows = b_ref[b_index].astype(jnp.float32)
        c_rows = c_ref[c_index]
        total = jnp.zeros((2 * edge, rank), jnp.float32)
        for start in range(0, edge, GROUP):
            pieces = []
            for row in range(start, start + GROUP):
                spread = jnp.broadcast_to(b_rows[row : row + 1], (16, rank)).astype(jnp.bfloat16)
                for low in range(0, edge, 16):
                    pieces.append(spread * c_rows[low : low + 16])
            khatri = jnp.concatenate(pieces, axis=0)
            columns = slice(start * edge, (start + GROUP) * edge)
            part = jnp.concatenate([held[one, :, columns], held[two, :, columns]], axis=0)
            total += jnp.dot(part, khatri, preferred_element_type=jnp.float32)
        return total.astype(jnp.bfloat16)

    def finish(index, term):
        one, two = first[index], second[index]
        code = ((coords[1, one] << low_bits | coords[2, one]) << 1 | 1).astype(jnp.float32)
        put(one, code, term[:edge])
        put(two, code, term[edge:])

    def await_pass(index):
        one, two = first[index], second[index]

        @pl.when(index + AHEAD < passes)
        def _():
            fetch_pass(index + AHEAD)

        fetch(one).wait()

        @pl.when(one != two)
        def _():
            fetch(two).wait()

    def run(together, begin):
        def step(trip, carry):
            indices = [begin + trip * together + i for i in range(together)]
            for index in indices:
                await_pass(index)
            for index, term in [(index, multiply(index)) for index in indices]:
                finish(index, term)
            return carry

        trips = lax.div(passes - begin, together)
        lax.fori_loop(0, trips, step, 0)
        return begin + trips * together

    begin = 0
    for together in TOGETHER:
        begin = run(together, begin)
    keep_ref[half * edge : half * edge + half, :] = codes[:half].astype(jnp.bfloat16)
    send_ref[half * edge : half * edge + half, :] = codes[half:].astype(jnp.bfloat16)


def own_terms(order, blocks, b_blocks, c_blocks, coords, count, total_rows):
    slots, edge, width = blocks.shape
    rank = b_blocks.shape[2]
    half = jax.ShapeDtypeStruct((total_rows // 2 * edge + padded(total_rows // 2), rank), jnp.bfloat16)
    vmem = pl.BlockSpec(memory_space=pltpu.VMEM)
    hbm = pl.BlockSpec(memory_space=pltpu.HBM)
    in_hbm = functools.partial(pltpu.with_memory_space_constraint, memory_space=pltpu.HBM)
    return pl.pallas_call(
        functools.partial(terms_kernel, order),
        out_shape=(half, half),
        in_specs=[hbm, pl.BlockSpec(memory_space=pl.ANY), hbm, hbm, hbm],
        out_specs=(vmem, vmem),
        scratch_shapes=[
            pltpu.VMEM((slots, edge, width), blocks.dtype),
            pltpu.VMEM(b_blocks.shape, b_blocks.dtype),
            pltpu.VMEM(c_blocks.shape, c_blocks.dtype),
            pltpu.SemaphoreType.DMA((slots,)),
            pltpu.SemaphoreType.DMA((4,)),
            pltpu.SMEM((3, slots), jnp.int32),
            pltpu.SMEM((1,), jnp.int32),
            pltpu.VMEM((total_rows, rank), jnp.float32),
            pltpu.SMEM((b_blocks.shape[0] * c_blocks.shape[0],), jnp.int32),
            pltpu.SMEM((slots + 1,), jnp.int32),
            pltpu.SMEM((slots + 1,), jnp.int32),
        ],
        compiler_params=pltpu.CompilerParams(vmem_limit_bytes=52 * MIB),
        cost_estimate=pl.CostEstimate(
            flops=slots * edge * width * rank * 2,
            bytes_accessed=slots * edge * width * 2,
            transcendentals=0,
        ),
        name="own_terms",
    )(in_hbm(coords.T), count, *(in_hbm(operand) for operand in (blocks, b_blocks, c_blocks)))


def grams_kernel(*refs):
    gram_ref = refs[-1]
    edge = refs[0].shape[1]
    place = 0
    for ref in refs[:-1]:
        for block in range(ref.shape[0]):
            rows = ref[block]
            gram_ref[place] = lax.dot_general(
                rows, rows, (((0,), (0,)), ((), ())), preferred_element_type=jnp.float32
            )
            place += 1
    del edge


def grams_of(parts):
    rank = parts[0].shape[2]
    edge = parts[0].shape[1]
    number = sum(p.shape[0] for p in parts)
    vmem = pl.BlockSpec(memory_space=pltpu.VMEM)
    return pl.pallas_call(
        grams_kernel,
        out_shape=jax.ShapeDtypeStruct((number, rank, rank), jnp.float32),
        in_specs=[vmem] * len(parts),
        out_specs=vmem,
        compiler_params=pltpu.CompilerParams(vmem_limit_bytes=(number * rank * rank * 4 + 6 * MIB)),
        cost_estimate=pl.CostEstimate(
            flops=number * edge * rank * rank * 2,
            bytes_accessed=number * edge * rank * 2,
            transcendentals=0,
        ),
        name="grams",
    )(*parts)


def split3(value):
    high = value.astype(jnp.bfloat16)
    rest = value - high.astype(jnp.float32)
    middle = rest.astype(jnp.bfloat16)
    return high, middle, (rest - middle.astype(jnp.float32)).astype(jnp.bfloat16)


def solve_kernel(shape, moment_ref, gram_b, early_c, late_c, out_ref, system, parts, work, b_list, c_list, remaining):
    size_ja, size_ka, second_dev, third_dev, b_place, c_place, last = shape
    edge, rank = out_ref.shape
    sources = size_ja * size_ka
    lanes = lax.broadcasted_iota(jnp.int32, (1, rank), 1)
    core = lax.axis_index("ja") & 1

    low_bits = (third_dev - 1).bit_length()
    width = low_bits + (second_dev - 1).bit_length() + 1
    per = 24 // width
    weight = jnp.left_shift(1, width * lax.rem(lanes, per)).astype(jnp.float32)
    weighted = moment_ref[edge : edge + 1, :] * weight
    packed = [
        jnp.sum(jnp.where(lax.div(lanes, per) == group, weighted, 0.0)).astype(jnp.int32)
        for group in range(pl.cdiv(sources, per))
    ]
    half = third_dev // 2
    live = [0, 0]
    for source in range(sources):
        number, offset = c_place[source % size_ka]
        late = int(number == last)
        code = lax.shift_right_logical(packed[source // per], width * (source % per)) & ((1 << width) - 1)
        field = lax.shift_right_logical(code, 1)
        second, third = lax.shift_right_logical(field, low_bits), field & ((1 << low_bits) - 1)
        upper = (third >= half).astype(jnp.int32)
        far = jnp.bitwise_xor(upper, core)
        block = (0 if late else number) * 2 * third_dev + (far * 2 + offset) * half + third - upper * half
        b_list[late, live[late]] = b_place[source // size_ka] * second_dev + second
        c_list[late, live[late]] = block
        live[late] = live[late] + (code & 1)

    strip = min(STRIP, rank)
    for low in range(0, rank, strip):
        rows = lax.broadcasted_iota(jnp.int32, (strip, rank), 0) + low
        columns = lax.broadcasted_iota(jnp.int32, (strip, rank), 1)

        total = jnp.where(rows == columns, RIDGE, 0.0)
        for late, gram_c in enumerate((early_c, late_c)):

            def product(index, late=late, gram_c=gram_c, low=low):
                left = gram_b[b_list[late, index], low : low + strip, :]
                return left * gram_c[c_list[late, index], low : low + strip, :]

            def add_two(trip, total, product=product):
                return total + product(2 * trip) + product(2 * trip + 1)

            def add(index, total, product=product):
                return total + product(index)

            paired = lax.shift_right_logical(live[late], 1)
            total = lax.fori_loop(0, paired, add_two, total)
            total = lax.fori_loop(2 * paired, live[late], add, total)
        system[low : low + strip] = total
        for place, part in enumerate(split3(total)):
            parts[place, low : low + strip] = part

    eye = lax.broadcasted_iota(jnp.int32, (rank, rank), 0) == lax.broadcasted_iota(jnp.int32, (rank, rank), 1)
    inverse = 1.0 / jnp.sum(jnp.where(eye, system[...], 0.0), axis=0, keepdims=True)
    moment = moment_ref[:edge, :]
    remaining[0] = 0
    scale = jnp.max(jnp.abs(moment), axis=1, keepdims=True)
    goal = moment / jnp.where(scale > 0, scale, 1.0)
    limit = TOLERANCE * TOLERANCE * jnp.sum(goal * goal, axis=1, keepdims=True)

    def times_system(value):
        high, middle, low = split3(value)
        three = jnp.dot(
            jnp.concatenate([high, middle, low], axis=0), parts[0], preferred_element_type=jnp.float32
        )
        two = jnp.dot(jnp.concatenate([high, middle], axis=0), parts[1], preferred_element_type=jnp.float32)
        one = jnp.dot(high, parts[2], preferred_element_type=jnp.float32)
        small = (one + two[edge:]) + three[2 * edge :]
        return three[:edge] + ((two[:edge] + three[edge : 2 * edge]) + small)

    def row_sum(value):
        return jnp.sum(value, axis=1, keepdims=True)

    def ratio(over, under):
        return jnp.where(under > 0, over / jnp.where(under > 0, under, 1.0), 0.0)

    def excess(r):
        return jnp.max(row_sum(r * r) - limit)

    x, r, p, s = jnp.zeros_like(goal), goal, jnp.zeros_like(goal), jnp.zeros_like(goal)
    old_gamma = alpha = None
    for _ in range(FIXED_STEPS):
        z = r * inverse
        q = times_system(z)
        gamma, delta = row_sum(r * z), row_sum(q * z)
        if alpha is None:
            p, s, curvature = z, q, delta
        else:
            beta = ratio(gamma, old_gamma)
            p, s = z + beta * p, q + beta * s
            curvature = delta - beta * ratio(gamma, alpha)
        old_gamma, alpha = gamma, ratio(gamma, curvature)
        x, r = x + alpha * p, r - alpha * s
    out_ref[...] = x * scale

    @pl.when(jnp.logical_not(excess(r) <= 0))
    def _():
        def advance(state):
            x, r, p, rz = state
            q = times_system(p)
            alpha = ratio(rz, row_sum(p * q))
            x, r = x + alpha * p, r - alpha * q
            z = r * inverse
            new_rz = row_sum(r * z)
            return x, r, z + ratio(new_rz, rz) * p, new_rz

        def unfinished(carry):
            return (carry[0] < MOST_STEPS) & (carry[1] > 0)

        def more(carry):
            following = advance(carry[2])
            return carry[0] + 1, excess(following[1]), following

        r = goal - times_system(x)
        z = r * inverse
        _, left, state = lax.while_loop(unfinished, more, (0, excess(r), (x, r, z, row_sum(r * z))))
        out_ref[...] = state[0] * scale
        remaining[0] = jnp.where(left <= 0, 0, 1)

    @pl.when(remaining[0] > 0)
    def _():
        work[:rank] = system[...]
        work[rank:] = goal

        def sweep(column, carry):
            row = work[pl.ds(column, 1), :]
            pivot = jnp.sum(jnp.where(lanes == column, row, 0.0), axis=1, keepdims=True)
            current = work[...]
            factor = jnp.sum(jnp.where(lanes == column, current, 0.0), axis=1, keepdims=True) / pivot
            work[...] = jnp.where(lanes == column, factor, current - factor * row)
            return carry

        lax.fori_loop(0, rank, sweep, 0)
        out_ref[...] = work[rank:] * scale


def solve(shape, moment, gram_b, gram_c, edge):
    rank = moment.shape[-1]
    sources = shape[0] * shape[1]
    vmem = pl.BlockSpec(memory_space=pltpu.VMEM)
    return pl.pallas_call(
        functools.partial(solve_kernel, shape),
        out_shape=jax.ShapeDtypeStruct((edge, rank), jnp.float32),
        in_specs=[vmem] * 4,
        out_specs=vmem,
        scratch_shapes=[
            pltpu.VMEM((rank, rank), jnp.float32),
            pltpu.VMEM((3, rank, rank), jnp.bfloat16),
            pltpu.VMEM((rank + edge, rank), jnp.float32),
            pltpu.SMEM((2, sources + 1), jnp.int32),
            pltpu.SMEM((2, sources + 1), jnp.int32),
            pltpu.SMEM((1,), jnp.int32),
        ],
        compiler_params=pltpu.CompilerParams(
            vmem_limit_bytes=(gram_b.size + sum(c.size for c in gram_c)) * 4 + 8 * MIB
        ),
        name="solve",
    )(moment, gram_b, *gram_c)


def body(blocks, factor_b, factor_c, block_coords, block_count):
    edge = blocks.shape[1]
    rank = factor_b.shape[1]
    size_ja, size_ka = lax.axis_size("ja"), lax.axis_size("ka")
    devices = size_ja * size_ka
    second_dev = factor_b.shape[0] // edge
    third_dev = factor_c.shape[0] // edge
    assert devices & (devices - 1) == 0 and size_ja >= 2 and devices <= rank
    assert second_dev * third_dev <= 64 and third_dev % 2 == 0
    plan = stage_plan(size_ja, size_ka)
    order = [bit for group in reversed(plan) for bit in group]
    core = lax.axis_index("ja") & 1
    b_blocks = factor_b.reshape(second_dev, edge, rank)
    c_blocks = factor_c.reshape(third_dev, edge, rank)
    core_mask = size_ka

    b_parts, b_place, held = [b_blocks], [0] * size_ja, [0]
    for bit in list(range(1, size_ja.bit_length() - 1)) + [0]:
        b_parts = b_parts + [xor_permute(part, size_ka << bit) for part in b_parts]
        held = held + [q ^ (1 << bit) for q in held]
    for place, q in enumerate(held):
        b_place[q] = place
    c_place = [0] * size_ka
    c_near = xor_permute(c_blocks, 1)
    halves = [lax.dynamic_slice_in_dim(c, core * (third_dev // 2), third_dev // 2, 0) for c in (c_blocks, c_near)]
    c_sets = [jnp.concatenate(halves, axis=0)]
    starts = [0]
    for bit in range(size_ka.bit_length() - 2, 0, -1):
        for number in range(len(c_sets)):
            c_sets.append(xor_permute(c_sets[number], 1 << bit))
        starts = starts + [q ^ (1 << bit) for q in starts]
    for number, q in enumerate(starts):
        c_place[q], c_place[q ^ 1] = (number, 0), (number, 1)
    c_other = []
    for number, part in enumerate(c_sets):
        c_other.append(xor_permute(part, core_mask))
    gram_b = grams_of(b_parts)
    c_pairs = [[part, other] for part, other in zip(c_sets, c_other)]
    gram_c = [grams_of(sum(c_pairs[:-1], []))]
    gram_c.append(grams_of(c_pairs[-1]))

    keep, send = own_terms(order, blocks, b_blocks, c_blocks, block_coords, block_count, devices)
    received = xor_permute(send, core_mask)
    total = keep.astype(jnp.float32) + received.astype(jnp.float32)
    rows = devices // 2
    for group in plan[1:]:
        rows >>= len(group)
        number = 1 << len(group)
        terms = [total[rows * edge * piece : rows * edge * (piece + 1)] for piece in range(number)]
        first_code = rows * number * edge
        codes = [total[first_code + rows * piece : first_code + rows * (piece + 1)] for piece in range(number)]
        spare = ((0, padded(rows) - rows), (0, 0))
        messages = [jnp.concatenate([part, jnp.pad(code, spare)], axis=0) for part, code in zip(terms, codes)]
        arrived = []
        for piece in range(1, number):
            mask = sum(1 << bit for i, bit in enumerate(group) if piece >> i & 1)
            arrived.append(xor_permute(messages[piece].astype(jnp.bfloat16), mask))
        total = messages[0]
        for part in arrived:
            total = total + part.astype(jnp.float32)
    shape = (size_ja, size_ka, second_dev, third_dev, tuple(b_place), tuple(c_place), len(c_sets) - 1)
    return solve(shape, total, gram_b, gram_c, edge)


def solution(mesh):
    placed = (P(ALL, None, None), P("ja", None), P("ka", None), P(ALL, None), P(ALL))
    return jax.shard_map(body, mesh=mesh, in_specs=placed, out_specs=P(ALL, None), check_vma=False)
```
